128 devices in a mesh: row: 16 (over x, y_hi, core), col: 8 (over z, y_lo).
Axes of the slice: x: 4, y: 4 (y_hi: 2, y_lo: 2; y = y_hi * 2 + y_lo), z: 4, core: 2. Of those that a mesh axis runs over, the one named last changes fastest.
Arguments:
- database: bfloat16 [8192, 32768], P('row', 'col'), may hold values from -1 to 1
- query: bfloat16 [256, 8192], P('col', 'row'), may hold values from -8 to 8
- slot_map: int32 [256], replicated, may hold values from 0 to 255, each once
- keys: bfloat16 [256, 2048, 512], P(('row', 'col')), may hold values from -0.125 to 0.125
Outputs:
- packed: float32 [256, 16, 512], P(('row', 'col'))
The draws below stay inside these ranges and needn't reach their ends.
Inputs may be any that keep to these rules, and one draw needn't show every extreme that they name: `slot_map`: each slot serves a different client.
All inputs are finite; a program needn't handle non-finite values.
Results may differ from the reference program's by a relative error of at most 0.0085.
Values may be sent and summed in bfloat16 or wider, within the bound.
A program may use at most 64 MiB of HBM per device.

```python
import jax
import jax.numpy as jnp
from jax import lax

TILE = 2048
PACK = 512
QUERIES = 256
DBROWS = 8192
DBCOLS = 32768


def draw_query(key, part):
    first = jax.random.fold_in(jax.random.fold_in(key, 11), 0)
    base = jax.random.normal(first, (QUERIES, DBROWS), jnp.float32)
    values = jnp.clip(base, -8.0, 8.0)
    return values.astype(jnp.bfloat16)


def shard_levels(own_key, shape, pieces, least, largest):
    gain = 1.0
    for dim, shards_of in pieces:
        steps = jax.random.uniform(jax.random.fold_in(jax.random.fold_in(own_key, 6), dim), (shards_of,), jnp.float32, least / len(pieces), largest / len(pieces))
        gain = gain * jnp.repeat(jnp.exp(steps), shape[dim] // shards_of).reshape((-1,) + (1,) * (len(shape) - 1 - dim))
    return gain


def normal_values(own_key, shape, spread, reach, cuts=(), dtype=jnp.bfloat16):
    array = spread * jax.random.normal(own_key, shape, jnp.float32)
    if cuts:
        array = array * shard_levels(own_key, shape, cuts, -0.22, 0.18)
    return jnp.clip(array, -reach, reach).astype(dtype)


def setup_inputs(seed: int = 0) -> dict:
    streams_of = jax.random.split(jax.random.key(seed), 5)
    database = jnp.clip(jax.random.uniform(streams_of[0], (DBROWS, DBCOLS), jnp.float32, -1.0, 1.0) * shard_levels(streams_of[0], (DBROWS, DBCOLS), ((0, 16), (1, 8)), -0.4, 0.0), -1.0, 1.0).astype(jnp.bfloat16)
    query = draw_query(jax.random.fold_in(streams_of[4], 71), 0)
    slot_map = jax.random.permutation(streams_of[2], QUERIES).astype(jnp.int32)
    keys = normal_values(streams_of[3], (QUERIES, TILE, PACK), TILE ** -0.5, 0.125, ((0, 128),))
    return dict(database=database, query=query, slot_map=slot_map, keys=keys)


def pack_slot(pair):
    tiles, block = pair
    return jnp.dot(tiles.astype(jnp.float32), block.astype(jnp.float32), preferred_element_type=jnp.float32)


def reference(database, query, slot_map, keys):
    chosen = jnp.take(query, slot_map, axis=0)
    answers = jnp.dot(chosen, database, preferred_element_type=jnp.float32)
    switched = (answers * (float(DBROWS) ** -0.5)).astype(jnp.bfloat16)
    tiles = switched.reshape(switched.shape[0], -1, TILE)
    return lax.map(pack_slot, (tiles, keys))
```

```python
import functools

import jax
import jax.numpy as jnp
from jax import lax
from jax.experimental import pallas as pl
from jax.experimental.pallas import tpu as pltpu
from jax.sharding import PartitionSpec as P

MESH = pl.DeviceIdType.MESH
CHUNKS = 4
F32 = jnp.float32
BF16 = jnp.bfloat16


def place():
    row, col = lax.axis_index("row"), lax.axis_index("col")
    x, y_hi, core = row // 4, lax.rem(row // 2, 2), lax.rem(row, 2)
    z, y_lo = col // 2, lax.rem(col, 2)
    return x, 2 * y_hi + y_lo, z, core


def device(x, y, z, core):
    x, y, z = lax.rem(x, 4), lax.rem(y, 4), lax.rem(z, 4)
    return ((2 * x + y // 2) * 2 + core, 2 * z + lax.rem(y, 2))


def kernel(
    factor,
    slot_hbm,
    query_hbm,
    db_hbm,
    keys_hbm,
    out_ref,
    slots,
    gathered,
    db,
    keys,
    core_out,
    core_in,
    own,
    far_out,
    far_in,
    near_out,
    near_in,
    spread,
    send_out,
    arrived,
    switched,
    local_sem,
    db_sem,
    keys_sem,
    query_sems,
    core_sems,
    far_sems,
    near_sems,
    owner_sems,
):
    x, y, z, core = place()
    y_hi, y_lo = y // 2, lax.rem(y, 2)
    col = 2 * z + y_lo
    depth = keys_hbm.shape[1] // CHUNKS
    lane_groups = depth // 128

    def remote(src, dst, sems, index, target):
        return pltpu.make_async_remote_copy(
            src_ref=src,
            dst_ref=dst,
            send_sem=sems.at[(0, *index)],
            recv_sem=sems.at[(1, *index)],
            device_id=target,
            device_id_type=MESH,
        )

    slot_copy = pltpu.make_async_copy(slot_hbm, slots, local_sem.at[0])
    slot_copy.start()
    own_query = pltpu.make_async_copy(query_hbm, gathered.at[col], local_sem.at[1])
    own_query.start()
    db_copies = []
    for k in range(CHUNKS):
        for t in range(2):
            start = t * keys_hbm.shape[1] + k * depth
            copy = pltpu.make_async_copy(
                db_hbm.at[:, pl.ds(start, depth)],
                db.at[k, :, pl.ds(t * depth, depth)],
                db_sem.at[k, t],
            )
            copy.start()
            db_copies.append(copy)
    key_copies = []
    for k in range(CHUNKS):
        copy = pltpu.make_async_copy(
            keys_hbm.at[:, pl.ds(k * depth, depth), :], keys.at[k], keys_sem.at[k]
        )
        copy.start()
        key_copies.append(copy)

    partner = device(x, y, z, 1 - core)
    right, left = device(x + 1, y, z, core), device(x + 3, y, z, core)
    owners = [device(x, y + b // 4, z + b % 4, core) for b in range(16)]
    column_peers = []
    for other in range(2):
        peer_y = 2 * y_hi + (y_lo if other == 0 else 1 - y_lo)
        for dz in (2, 1, 3, 0):
            if other or dz:
                column_peers.append(device(x, peer_y, z + dz, core))

    barrier = pltpu.get_barrier_semaphore()
    greeted = [partner, right, left, *owners[1:]]
    for target in greeted:
        pl.semaphore_signal(barrier, inc=1, device_id=target, device_id_type=MESH)
    pl.semaphore_wait(barrier, len(greeted))

    query_copies = []
    for i, target in enumerate(column_peers):
        copy = remote(query_hbm, gathered.at[col], query_sems, (i,), target)
        copy.start()
        query_copies.append(copy)

    slot_copy.wait()
    total = slots.shape[1]
    line = lax.broadcasted_iota(jnp.int32, (total, total), 0)
    place_at = lax.broadcasted_iota(jnp.int32, (total, total), 1)
    to_core = (line >> 7) + core & 1
    to_x = (line >> 5) + x & 3
    part = line >> 4 & 1
    to_y = (line >> 2) + y & 3
    to_z = line + z & 3
    owner_row = (to_x * 2 + (to_y >> 1)) * 2 + to_core
    owner_col = to_z * 2 + (to_y & 1)
    slot_of_line = (owner_row * 8 + owner_col) * 2 + part
    line_is_slot = jnp.where(slot_of_line == place_at, 1.0, 0.0).astype(BF16)
    client_at_slot = jnp.broadcast_to(slots[...], (total, total))
    client_is_slot = jnp.where(client_at_slot == line, 1.0, 0.0).astype(BF16)
    chooser = lax.dot_general(
        line_is_slot, client_is_slot, (((1,), (1,)), ((), ())), preferred_element_type=F32
    ).astype(BF16)

    own_query.wait()
    for copy in query_copies:
        copy.wait_recv()
    entries = gathered[...].reshape(total, query_hbm.shape[1])
    chosen = jnp.dot(chooser, entries, preferred_element_type=F32).astype(BF16)
    half = total // 2

    sent = list(query_copies)
    core_copies, far_copies, near_copies, owner_copies = {}, {}, {}, {}

    def multiply(k):
        db_copies[2 * k].wait()
        db_copies[2 * k + 1].wait()
        block = db[k]
        core_out[k] = jnp.dot(chosen[half:], block, preferred_element_type=F32).astype(BF16)
        copy = remote(core_out.at[k], core_in.at[k], core_sems, (k,), partner)
        copy.start()
        core_copies[k] = copy
        own[k] = jnp.dot(chosen[:half], block, preferred_element_type=F32)

    def start_near(k, side, lines):
        target = (right, left)[side]
        copy = remote(
            near_out.at[k, side, lines],
            near_in.at[k, side, lines],
            near_sems,
            (k, side, lines),
            target,
        )
        copy.start()
        near_copies[k, side, lines] = copy

    def halve(k):
        core_copies[k].wait_recv()
        for side in range(2):
            lines = pl.ds(64 + 16 * side, 16)
            far_out[k, side] = (own[k, lines] + core_in[k, lines].astype(F32)).astype(BF16)
            copy = remote(
                far_out.at[k, side], far_in.at[k, side], far_sems, (k, side), (right, left)[side]
            )
            copy.start()
            far_copies[k, side] = copy
        for side in range(2):
            lines = pl.ds((48, 96)[side], 16)
            near_out[k, side, 1 - side] = (
                own[k, lines] + core_in[k, lines].astype(F32)
            ).astype(BF16)
            start_near(k, side, 1 - side)
        for lines in (pl.ds(32, 16), pl.ds(112, 16), pl.ds(0, 32)):
            own[k, lines] = own[k, lines] + core_in[k, lines].astype(F32)

    def pass_on(k):
        for side in range(2):
            far_copies[k, side].wait_recv()
            lines = pl.ds((32, 112)[side], 16)
            near_out[k, side, side] = (own[k, lines] + far_in[k, side].astype(F32)).astype(BF16)
            start_near(k, side, side)

    def to_owners(k):
        for part in range(2):
            for side in range(2):
                near_copies[k, side, part].wait_recv()
            lines = pl.ds(16 * part, 16)
            summed = (
                own[k, lines] + near_in[k, 0, part].astype(F32) + near_in[k, 1, part].astype(F32)
            )
            for t in range(2):
                for g in range(lane_groups):
                    lane = t * depth + g * 128
                    at = t * 2 * lane_groups + part * lane_groups + g
                    spread[pl.ds(at, 16, stride=16), :] = summed[:, lane : lane + 128]
        send_out[k] = spread[...].astype(BF16).reshape(send_out.shape[1:])
        landing = arrived.at[k, y_hi, col]
        pltpu.make_async_copy(send_out.at[k, 0], landing, owner_sems.at[1, k]).start()
        for b in range(1, 16):
            remote(send_out.at[k, b], landing, owner_sems, (k,), owners[b]).start()

    totals = [None, None]

    def pack(k):
        pltpu.make_async_copy(arrived.at[k], arrived.at[k], owner_sems.at[1, k]).wait()
        key_copies[k].wait()
        both = arrived[k, 0].astype(F32) + arrived[k, 1].astype(F32)
        switched[...] = (both * factor).reshape(switched.shape)
        for part in range(2):
            pieces = [
                switched[pl.ds(part * lane_groups + g, 16, stride=4 * lane_groups // 2), :]
                for g in range(lane_groups)
            ]
            tiles = jnp.concatenate(pieces, axis=1).astype(BF16)
            product = jnp.dot(tiles, keys[k, part], preferred_element_type=F32)
            totals[part] = product if totals[part] is None else totals[part] + product

    multiply(0)
    multiply(1)
    halve(0)
    multiply(2)
    halve(1)
    multiply(3)
    halve(2)
    pass_on(0)
    halve(3)
    pass_on(1)
    pass_on(2)
    to_owners(0)
    pass_on(3)
    to_owners(1)
    to_owners(2)
    pack(0)
    to_owners(3)
    pack(1)
    pack(2)
    pack(3)
    for part in range(2):
        out_ref[part] = totals[part]

    for copies in (core_copies, far_copies, near_copies):
        sent.extend(copies.values())
    for copy in sent:
        copy.wait_send()
    for k in range(CHUNKS):
        block = send_out.at[k, pl.ds(1, 15)]
        pltpu.make_async_copy(block, block, owner_sems.at[0, k]).wait()


def shards(database, query, slot_map, keys):
    rows_axis = lax.axis_size("row")
    factor = float(database.shape[0] * rows_axis) ** (-0.5)
    total = slot_map.shape[0]
    rows, columns = database.shape
    tile, packs = keys.shape[1:]
    width = columns // CHUNKS
    half = total // 2
    dma = pltpu.SemaphoreType.DMA
    return pl.pallas_call(
        functools.partial(kernel, factor),
        out_shape=jax.ShapeDtypeStruct((2, 16, packs), F32),
        in_specs=[pl.BlockSpec(memory_space=pltpu.HBM)] * 4,
        out_specs=pl.BlockSpec(memory_space=pltpu.VMEM),
        scratch_shapes=[
            pltpu.VMEM((1, total), jnp.int32),
            pltpu.VMEM((8, total // 8, rows), BF16),
            pltpu.VMEM((CHUNKS, rows, width), BF16),
            pltpu.VMEM((CHUNKS, 2, tile // CHUNKS, packs), BF16),
            pltpu.VMEM((CHUNKS, half, width), BF16),
            pltpu.VMEM((CHUNKS, half, width), BF16),
            pltpu.VMEM((CHUNKS, half, width), F32),
            pltpu.VMEM((CHUNKS, 2, 16, width), BF16),
            pltpu.VMEM((CHUNKS, 2, 16, width), BF16),
            pltpu.VMEM((CHUNKS, 2, 2, 16, width), BF16),
            pltpu.VMEM((CHUNKS, 2, 2, 16, width), BF16),
            pltpu.VMEM((256, 128), F32),
            pltpu.VMEM((CHUNKS, 16, 16, 128), BF16),
            pltpu.VMEM((CHUNKS, 2, 8, 16, 128), BF16),
            pltpu.VMEM((128, 128), F32),
            dma((2,)),
            dma((CHUNKS, 2)),
            dma((CHUNKS,)),
            dma((2, 7)),
            dma((2, CHUNKS)),
            dma((2, CHUNKS, 2)),
            dma((2, CHUNKS, 2, 2)),
            dma((2, CHUNKS)),
        ],
        compiler_params=pltpu.CompilerParams(
            collective_id=1, has_side_effects=True, vmem_limit_bytes=40 * 1024 * 1024
        ),
        name="answer_and_pack",
    )(slot_map.reshape(1, total), query, database, keys)


def solution(mesh):
    return jax.shard_map(
        shards,
        mesh=mesh,
        in_specs=(P("row", "col"), P("col", "row"), P(), P(("row", "col"), None, None)),
        out_specs=P(("row", "col"), None, None),
        check_vma=False,
    )
```

```python
import functools

import jax
import jax.numpy as jnp
from jax import lax
from jax.experimental import pallas as pl
from jax.experimental.pallas import tpu as pltpu
from jax.sharding import PartitionSpec as P

MESH = pl.DeviceIdType.MESH
CHUNKS = 4
F32 = jnp.float32
BF16 = jnp.bfloat16


def place():
    row, col = lax.axis_index("row"), lax.axis_index("col")
    x, y_hi, core = row // 4, lax.rem(row // 2, 2), lax.rem(row, 2)
    z, y_lo = col // 2, lax.rem(col, 2)
    return x, 2 * y_hi + y_lo, z, core


def device(x, y, z, core):
    x, y, z = lax.rem(x, 4), lax.rem(y, 4), lax.rem(z, 4)
    return ((2 * x + y // 2) * 2 + core, 2 * z + lax.rem(y, 2))


def kernel(
    factor,
    slot_hbm,
    query_hbm,
    db_hbm,
    keys_hbm,
    out_ref,
    slots,
    gathered,
    db,
    keys,
    core_out,
    core_in,
    own,
    far_out,
    far_in,
    near_out,
    near_in,
    spread,
    send_out,
    arrived,
    switched,
    local_sem,
    db_sem,
    keys_sem,
    query_sems,
    core_sems,
    far_sems,
    near_sems,
    owner_sems,
):
    x, y, z, core = place()
    y_hi, y_lo = y // 2, lax.rem(y, 2)
    col = 2 * z + y_lo
    depth = keys_hbm.shape[1] // CHUNKS
    lane_groups = depth // 128

    def remote(src, dst, sems, index, target):
        return pltpu.make_async_remote_copy(
            src_ref=src,
            dst_ref=dst,
            send_sem=sems.at[(0, *index)],
            recv_sem=sems.at[(1, *index)],
            device_id=target,
            device_id_type=MESH,
        )

    slot_copy = pltpu.make_async_copy(slot_hbm, slots, local_sem.at[0])
    slot_copy.start()
    own_query = pltpu.make_async_copy(query_hbm, gathered.at[col], local_sem.at[1])
    own_query.start()
    db_copies = []
    for k in range(CHUNKS):
        for t in range(2):
            start = t * keys_hbm.shape[1] + k * depth
            copy = pltpu.make_async_copy(
                db_hbm.at[:, pl.ds(start, depth)],
                db.at[k, :, pl.ds(t * depth, depth)],
                db_sem.at[k, t],
            )
            copy.start()
            db_copies.append(copy)
    key_copies = []
    for k in range(CHUNKS):
        copy = pltpu.make_async_copy(
            keys_hbm.at[:, pl.ds(k * depth, depth), :], keys.at[k], keys_sem.at[k]
        )
        copy.start()
        key_copies.append(copy)

    partner = device(x, y, z, 1 - core)
    right, left = device(x + 1, y, z, core), device(x + 3, y, z, core)
    owners = [device(x, y + b // 4, z + b % 4, core) for b in range(16)]
    column_peers = []
    for other in range(2):
        peer_y = 2 * y_hi + (y_lo if other == 0 else 1 - y_lo)
        for dz in (2, 1, 3, 0):
            if other or dz:
                column_peers.append(device(x, peer_y, z + dz, core))

    barrier = pltpu.get_barrier_semaphore()
    greeted = [partner, right, left, *owners[1:]]
    for target in greeted:
        pl.semaphore_signal(barrier, inc=1, device_id=target, device_id_type=MESH)
    pl.semaphore_wait(barrier, len(greeted))

    query_copies = []
    for i, target in enumerate(column_peers):
        copy = remote(query_hbm, gathered.at[col], query_sems, (i,), target)
        copy.start()
        query_copies.append(copy)

    slot_copy.wait()
    total = slots.shape[1]
    line = lax.broadcasted_iota(jnp.int32, (total, total), 0)
    place_at = lax.broadcasted_iota(jnp.int32, (total, total), 1)
    to_core = (line >> 7) + core & 1
    to_x = (line >> 5) + x & 3
    part = line >> 4 & 1
    to_y = (line >> 2) + y & 3
    to_z = line + z & 3
    owner_row = (to_x * 2 + (to_y >> 1)) * 2 + to_core
    owner_col = to_z * 2 + (to_y & 1)
    slot_of_line = (owner_row * 8 + owner_col) * 2 + part
    line_is_slot = jnp.where(slot_of_line == place_at, 1.0, 0.0).astype(BF16)
    client_at_slot = jnp.broadcast_to(slots[...], (total, total))
    client_is_slot = jnp.where(client_at_slot == line, 1.0, 0.0).astype(BF16)
    chooser = lax.dot_general(
        line_is_slot, client_is_slot, (((1,), (1,)), ((), ())), preferred_element_type=F32
    ).astype(BF16)

    own_query.wait()
    for copy in query_copies:
        copy.wait_recv()
    entries = gathered[...].reshape(total, query_hbm.shape[1])
    chosen = jnp.dot(chooser, entries, preferred_element_type=F32).astype(BF16)
    half = total // 2

    sent = list(query_copies)
    core_copies, far_copies, near_copies, owner_copies = {}, {}, {}, {}

    def multiply(k):
        db_copies[2 * k].wait()
        db_copies[2 * k + 1].wait()
        block = db[k]
        core_out[k] = jnp.dot(chosen[half:], block, preferred_element_type=F32).astype(BF16)
        copy = remote(core_out.at[k], core_in.at[k], core_sems, (k,), partner)
        copy.start()
        core_copies[k] = copy
        own[k] = jnp.dot(chosen[:half], block, preferred_element_type=F32)

    def start_near(k, side, lines):
        target = (right, left)[side]
        copy = remote(
            near_out.at[k, side, lines],
            near_in.at[k, side, lines],
            near_sems,
            (k, side, lines),
            target,
        )
        copy.start()
        near_copies[k, side, lines] = copy

    def halve(k):
        core_copies[k].wait_recv()
        for side in range(2):
            lines = pl.ds(64 + 16 * side, 16)
            far_out[k, side] = (own[k, lines] + core_in[k, lines].astype(F32)).astype(BF16)
            copy = remote(
                far_out.at[k, side], far_in.at[k, side], far_sems, (k, side), (right, left)[side]
            )
            copy.start()
            far_copies[k, side] = copy
        for side in range(2):
            lines = pl.ds((48, 96)[side], 16)
            near_out[k, side, 1 - side] = (
                own[k, lines] + core_in[k, lines].astype(F32)
            ).astype(BF16)
            start_near(k, side, 1 - side)
        for lines in (pl.ds(32, 16), pl.ds(112, 16), pl.ds(0, 32)):
            own[k, lines] = own[k, lines] + core_in[k, lines].astype(F32)

    def pass_on(k):
        for side in range(2):
            far_copies[k, side].wait_recv()
            lines = pl.ds((32, 112)[side], 16)
            near_out[k, side, side] = (own[k, lines] + far_in[k, side].astype(F32)).astype(BF16)
            start_near(k, side, side)

    def to_owners(k):
        for part in range(2):
            for side in range(2):
                near_copies[k, side, part].wait_recv()
            lines = pl.ds(16 * part, 16)
            summed = (
                own[k, lines] + near_in[k, 0, part].astype(F32) + near_in[k, 1, part].astype(F32)
            )
            for t in range(2):
                for g in range(lane_groups):
                    lane = t * depth + g * 128
                    at = t * 2 * lane_groups + part * lane_groups + g
                    spread[pl.ds(at, 16, stride=16), :] = summed[:, lane : lane + 128]
        send_out[k] = spread[...].astype(BF16).reshape(send_out.shape[1:])
        landing = arrived.at[k, y_hi, col]
        pltpu.make_async_copy(send_out.at[k, 0], landing, owner_sems.at[1, k]).start()
        for b in range(1, 16):
            remote(send_out.at[k, b], landing, owner_sems, (k,), owners[b]).start()

    totals = [None, None]

    def pack(k):
        pltpu.make_async_copy(arrived.at[k], arrived.at[k], owner_sems.at[1, k]).wait()
        key_copies[k].wait()
        both = arrived[k, 0].astype(F32) + arrived[k, 1].astype(F32)
        switched[...] = (both * factor).reshape(switched.shape)
        for part in range(2):
            pieces = [
                switched[pl.ds(part * lane_groups + g, 16, stride=4 * lane_groups // 2), :]
                for g in range(lane_groups)
            ]
            tiles = jnp.concatenate(pieces, axis=1).astype(BF16)
            product = jnp.dot(tiles, keys[k, part], preferred_element_type=F32)
            totals[part] = product if totals[part] is None else totals[part] + product

    multiply(0)
    multiply(1)
    halve(0)
    multiply(2)
    halve(1)
    multiply(3)
    halve(2)
    pass_on(0)
    halve(3)
    pass_on(1)
    pass_on(2)
    to_owners(0)
    pass_on(3)
    to_owners(1)
    to_owners(2)
    pack(0)
    to_owners(3)
    pack(1)
    pack(2)
    pack(3)
    for part in range(2):
        out_ref[part] = totals[part]

    for copies in (core_copies, far_copies, near_copies):
        sent.extend(copies.values())
    for copy in sent:
        copy.wait_send()
    for k in range(CHUNKS):
        block = send_out.at[k, pl.ds(1, 15)]
        pltpu.make_async_copy(block, block, owner_sems.at[0, k]).wait()


def shards(database, query, slot_map, keys):
    rows_axis = lax.axis_size("row")
    factor = float(database.shape[0] * rows_axis) ** (-0.5)
    total = slot_map.shape[0]
    rows, columns = database.shape
    tile, packs = keys.shape[1:]
    width = columns // CHUNKS
    half = total // 2
    dma = pltpu.SemaphoreType.DMA
    return pl.pallas_call(
        functools.partial(kernel, factor),
        out_shape=jax.ShapeDtypeStruct((2, 16, packs), F32),
        in_specs=[pl.BlockSpec(memory_space=pltpu.HBM)] * 4,
        out_specs=pl.BlockSpec(memory_space=pltpu.VMEM),
        scratch_shapes=[
            pltpu.VMEM((1, total), jnp.int32),
            pltpu.VMEM((8, total // 8, rows), BF16),
            pltpu.VMEM((CHUNKS, rows, width), BF16),
            pltpu.VMEM((CHUNKS, 2, tile // CHUNKS, packs), BF16),
            pltpu.VMEM((CHUNKS, half, width), BF16),
            pltpu.VMEM((CHUNKS, half, width), BF16),
            pltpu.VMEM((CHUNKS, half, width), F32),
            pltpu.VMEM((CHUNKS, 2, 16, width), BF16),
            pltpu.VMEM((CHUNKS, 2, 16, width), BF16),
            pltpu.VMEM((CHUNKS, 2, 2, 16, width), BF16),
            pltpu.VMEM((CHUNKS, 2, 2, 16, width), BF16),
            pltpu.VMEM((256, 128), F32),
            pltpu.VMEM((CHUNKS, 16, 16, 128), BF16),
            pltpu.VMEM((CHUNKS, 2, 8, 16, 128), BF16),
            pltpu.VMEM((128, 128), F32),
            dma((2,)),
            dma((CHUNKS, 2)),
            dma((CHUNKS,)),
            dma((2, 7)),
            dma((2, CHUNKS)),
            dma((2, CHUNKS, 2)),
            dma((2, CHUNKS, 2, 2)),
            dma((2, CHUNKS)),
        ],
        compiler_params=pltpu.CompilerParams(
            collective_id=1, has_side_effects=True, vmem_limit_bytes=40 * 1024 * 1024
        ),
        name="answer_and_pack",
    )(*(pltpu.with_memory_space_constraint(a, pltpu.HBM) for a in (slot_map.reshape(1, total), query, database, keys)))


def solution(mesh):
    return jax.shard_map(
        shards,
        mesh=mesh,
        in_specs=(P("row", "col"), P("col", "row"), P(), P(("row", "col"), None, None)),
        out_specs=P(("row", "col"), None, None),
        check_vma=False,
    )
```

```python
import functools

import jax
import jax.numpy as jnp
from jax import lax
from jax.experimental import pallas as pl
from jax.experimental.pallas import tpu as pltpu
from jax.sharding import PartitionSpec as P

MESH = pl.DeviceIdType.MESH
CHUNKS = 4
F32 = jnp.float32
BF16 = jnp.bfloat16


def place():
    row, col = lax.axis_index("row"), lax.axis_index("col")
    x, y_hi, core = row // 4, lax.rem(row // 2, 2), lax.rem(row, 2)
    z, y_lo = col // 2, lax.rem(col, 2)
    return x, 2 * y_hi + y_lo, z, core


def device(x, y, z, core):
    x, y, z = lax.rem(x, 4), lax.rem(y, 4), lax.rem(z, 4)
    return ((2 * x + y // 2) * 2 + core, 2 * z + lax.rem(y, 2))


def kernel(
    factor,
    slot_hbm,
    query_hbm,
    db_hbm,
    keys_hbm,
    out_ref,
    slots,
    gathered,
    db,
    keys,
    core_out,
    core_in,
    own,
    far_out,
    far_in,
    near_out,
    near_in,
    spread,
    send_out,
    arrived,
    switched,
    local_sem,
    db_sem,
    keys_sem,
    query_sems,
    core_sems,
    far_sems,
    near_sems,
    owner_sems,
    across_sem,
):
    x, y, z, core = place()
    y_hi, y_lo = y // 2, lax.rem(y, 2)
    col = 2 * z + y_lo
    depth = keys_hbm.shape[1] // CHUNKS
    lane_groups = depth // 128

    def remote(src, dst, sems, index, target):
        return pltpu.make_async_remote_copy(
            src_ref=src,
            dst_ref=dst,
            send_sem=sems.at[(0, *index)],
            recv_sem=sems.at[(1, *index)],
            device_id=target,
            device_id_type=MESH,
        )

    partner = device(x, y, z, 1 - core)
    right, left = device(x + 1, y, z, core), device(x + 3, y, z, core)
    owners = [device(x, y + b // 4, z + b % 4, core) for b in range(16)]
    column_peers = []
    for dz, other in ((2, 1), (2, 0), (1, 1), (3, 1), (1, 0), (3, 0), (0, 1)):
        peer_y = 2 * y_hi + (1 - y_lo if other else y_lo)
        column_peers.append(device(x, peer_y, z + dz, core))
    across = device(x, y + 3 + 2 * y_lo, z, core)

    barrier = pltpu.get_barrier_semaphore()
    greeted = [*column_peers, across, partner, right, left]
    for target in greeted:
        pl.semaphore_signal(barrier, inc=1, device_id=target, device_id_type=MESH)
    pl.semaphore_wait(barrier, len(greeted))

    query_copies = []
    for i, target in enumerate(column_peers):
        copy = remote(query_hbm, gathered.at[col], query_sems, (i,), target)
        copy.start()
        query_copies.append(copy)

    slot_copy = pltpu.make_async_copy(slot_hbm, slots, local_sem.at[0])
    slot_copy.start()
    own_query = pltpu.make_async_copy(query_hbm, gathered.at[col], local_sem.at[1])
    own_query.start()
    db_copies = []
    for k in range(CHUNKS):
        for t in range(2):
            start = t * keys_hbm.shape[1] + k * depth
            copy = pltpu.make_async_copy(
                db_hbm.at[:, pl.ds(start, depth)],
                db.at[k, :, pl.ds(t * depth, depth)],
                db_sem.at[k, t],
            )
            copy.start()
            db_copies.append(copy)
    key_copies = []
    for k in range(CHUNKS):
        copy = pltpu.make_async_copy(
            keys_hbm.at[:, pl.ds(k * depth, depth), :], keys.at[k], keys_sem.at[k]
        )
        copy.start()
        key_copies.append(copy)

    slot_copy.wait()
    total = slots.shape[1]
    line = lax.broadcasted_iota(jnp.int32, (total, total), 0)
    place_at = lax.broadcasted_iota(jnp.int32, (total, total), 1)
    to_core = (line >> 7) + core & 1
    to_x = (line >> 5) + x & 3
    part = line >> 4 & 1
    to_y = (line >> 2) + y & 3
    to_z = line + z & 3
    owner_row = (to_x * 2 + (to_y >> 1)) * 2 + to_core
    owner_col = to_z * 2 + (to_y & 1)
    slot_of_line = (owner_row * 8 + owner_col) * 2 + part
    line_is_slot = jnp.where(slot_of_line == place_at, 1.0, 0.0).astype(BF16)
    client_at_slot = jnp.broadcast_to(slots[...], (total, total))
    client_is_slot = jnp.where(client_at_slot == line, 1.0, 0.0).astype(BF16)
    chooser = lax.dot_general(
        line_is_slot, client_is_slot, (((1,), (1,)), ((), ())), preferred_element_type=F32
    ).astype(BF16)

    own_query.wait()
    for copy in query_copies:
        copy.wait_recv()
    pl.semaphore_signal(across_sem, inc=1, device_id=across, device_id_type=MESH)
    entries = gathered[...].reshape(total, query_hbm.shape[1])
    chosen = jnp.dot(chooser, entries, preferred_element_type=F32).astype(BF16)
    half = total // 2

    sent = list(query_copies)
    core_copies, far_copies, near_copies, owner_copies = {}, {}, {}, {}

    def multiply(k):
        db_copies[2 * k].wait()
        db_copies[2 * k + 1].wait()
        block = db[k]
        core_out[k] = jnp.dot(chosen[half:], block, preferred_element_type=F32).astype(BF16)
        copy = remote(core_out.at[k], core_in.at[k], core_sems, (k,), partner)
        copy.start()
        core_copies[k] = copy
        own[k] = jnp.dot(chosen[:half], block, preferred_element_type=F32)

    def start_near(k, side, lines):
        target = (right, left)[side]
        copy = remote(
            near_out.at[k, side, lines],
            near_in.at[k, side, lines],
            near_sems,
            (k, side, lines),
            target,
        )
        copy.start()
        near_copies[k, side, lines] = copy

    def halve(k):
        core_copies[k].wait_recv()
        for side in range(2):
            lines = pl.ds(64 + 16 * side, 16)
            far_out[k, side] = (own[k, lines] + core_in[k, lines].astype(F32)).astype(BF16)
            copy = remote(
                far_out.at[k, side], far_in.at[k, side], far_sems, (k, side), (right, left)[side]
            )
            copy.start()
            far_copies[k, side] = copy
        for side in range(2):
            lines = pl.ds((48, 96)[side], 16)
            near_out[k, side, 1 - side] = (
                own[k, lines] + core_in[k, lines].astype(F32)
            ).astype(BF16)
            start_near(k, side, 1 - side)
        for lines in (pl.ds(32, 16), pl.ds(112, 16), pl.ds(0, 32)):
            own[k, lines] = own[k, lines] + core_in[k, lines].astype(F32)

    def pass_on(k):
        for side in range(2):
            far_copies[k, side].wait_recv()
            lines = pl.ds((32, 112)[side], 16)
            near_out[k, side, side] = (own[k, lines] + far_in[k, side].astype(F32)).astype(BF16)
            start_near(k, side, side)

    def to_owners(k):
        for part in range(2):
            for side in range(2):
                near_copies[k, side, part].wait_recv()
            lines = pl.ds(16 * part, 16)
            summed = (
                own[k, lines] + near_in[k, 0, part].astype(F32) + near_in[k, 1, part].astype(F32)
            )
            for t in range(2):
                for g in range(lane_groups):
                    lane = t * depth + g * 128
                    at = t * 2 * lane_groups + part * lane_groups + g
                    spread[pl.ds(at, 16, stride=4 * lane_groups), :] = summed[:, lane : lane + 128]
        send_out[k] = spread[...].astype(BF16).reshape(send_out.shape[1:])
        landing = arrived.at[k, y_hi, col]
        pltpu.make_async_copy(send_out.at[k, 0], landing, owner_sems.at[1, k]).start()
        for b in range(1, 16):
            remote(send_out.at[k, b], landing, owner_sems, (k,), owners[b]).start()

    totals = [None, None]

    def pack(k):
        pltpu.make_async_copy(arrived.at[k], arrived.at[k], owner_sems.at[1, k]).wait()
        key_copies[k].wait()
        both = arrived[k, 0].astype(F32) + arrived[k, 1].astype(F32)
        switched[...] = (both * factor).reshape(switched.shape)
        for part in range(2):
            pieces = [
                switched[pl.ds(part * lane_groups + g, 16, stride=2 * lane_groups), :]
                for g in range(lane_groups)
            ]
            tiles = jnp.concatenate(pieces, axis=1).astype(BF16)
            product = jnp.dot(tiles, keys[k, part], preferred_element_type=F32)
            totals[part] = product if totals[part] is None else totals[part] + product

    multiply(0)
    multiply(1)
    halve(0)
    multiply(2)
    halve(1)
    multiply(3)
    halve(2)
    pass_on(0)
    halve(3)
    pass_on(1)
    pass_on(2)
    pl.semaphore_wait(across_sem, 1)
    to_owners(0)
    pass_on(3)
    to_owners(1)
    to_owners(2)
    pack(0)
    to_owners(3)
    pack(1)
    pack(2)
    pack(3)
    for part in range(2):
        out_ref[part] = totals[part]

    for copies in (core_copies, far_copies, near_copies):
        sent.extend(copies.values())
    for copy in sent:
        copy.wait_send()
    for k in range(CHUNKS):
        block = send_out.at[k, pl.ds(1, 15)]
        pltpu.make_async_copy(block, block, owner_sems.at[0, k]).wait()


def shards(database, query, slot_map, keys):
    rows_axis = lax.axis_size("row")
    factor = float(database.shape[0] * rows_axis) ** (-0.5)
    total = slot_map.shape[0]
    rows, columns = database.shape
    tile, packs = keys.shape[1:]
    width = columns // CHUNKS
    half = total // 2
    dma = pltpu.SemaphoreType.DMA
    return pl.pallas_call(
        functools.partial(kernel, factor),
        out_shape=jax.ShapeDtypeStruct((2, 16, packs), F32),
        in_specs=[pl.BlockSpec(memory_space=pltpu.HBM)] * 4,
        out_specs=pl.BlockSpec(memory_space=pltpu.VMEM),
        scratch_shapes=[
            pltpu.VMEM((1, total), jnp.int32),
            pltpu.VMEM((8, total // 8, rows), BF16),
            pltpu.VMEM((CHUNKS, rows, width), BF16),
            pltpu.VMEM((CHUNKS, 2, tile // CHUNKS, packs), BF16),
            pltpu.VMEM((CHUNKS, half, width), BF16),
            pltpu.VMEM((CHUNKS, half, width), BF16),
            pltpu.VMEM((CHUNKS, half, width), F32),
            pltpu.VMEM((CHUNKS, 2, 16, width), BF16),
            pltpu.VMEM((CHUNKS, 2, 16, width), BF16),
            pltpu.VMEM((CHUNKS, 2, 2, 16, width), BF16),
            pltpu.VMEM((CHUNKS, 2, 2, 16, width), BF16),
            pltpu.VMEM((tile // CHUNKS // 128 * 64, 128), F32),
            pltpu.VMEM((CHUNKS, 16, tile // CHUNKS // 32, 128), BF16),
            pltpu.VMEM((CHUNKS, 2, 8, tile // CHUNKS // 32, 128), BF16),
            pltpu.VMEM((tile // CHUNKS // 128 * 32, 128), F32),
            dma((2,)),
            dma((CHUNKS, 2)),
            dma((CHUNKS,)),
            dma((2, 7)),
            dma((2, CHUNKS)),
            dma((2, CHUNKS, 2)),
            dma((2, CHUNKS, 2, 2)),
            dma((2, CHUNKS)),
            pltpu.SemaphoreType.REGULAR,
        ],
        compiler_params=pltpu.CompilerParams(
            collective_id=1, has_side_effects=True, vmem_limit_bytes=40 * 1024 * 1024
        ),
        name="answer_and_pack",
    )(*(pltpu.with_memory_space_constraint(a, pltpu.HBM) for a in (slot_map.reshape(1, total), query, database, keys)))


def solution(mesh):
    return jax.shard_map(
        shards,
        mesh=mesh,
        in_specs=(P("row", "col"), P("col", "row"), P(), P(("row", "col"), None, None)),
        out_specs=P(("row", "col"), None, None),
        check_vma=False,
    )
```

```python
import functools

import jax
import jax.numpy as jnp
from jax import lax
from jax.experimental import pallas as pl
from jax.experimental.pallas import tpu as pltpu
from jax.sharding import PartitionSpec as P

MESH = pl.DeviceIdType.MESH
CHUNKS = 4
F32 = jnp.float32
BF16 = jnp.bfloat16


def place():
    row, col = lax.axis_index("row"), lax.axis_index("col")
    x, y_hi, core = row // 4, lax.rem(row // 2, 2), lax.rem(row, 2)
    z, y_lo = col // 2, lax.rem(col, 2)
    return x, 2 * y_hi + y_lo, z, core


def device(x, y, z, core):
    x, y, z = lax.rem(x, 4), lax.rem(y, 4), lax.rem(z, 4)
    return ((2 * x + y // 2) * 2 + core, 2 * z + lax.rem(y, 2))


def kernel(
    factor,
    slot_hbm,
    query_hbm,
    db_hbm,
    keys_hbm,
    out_ref,
    slots,
    gathered,
    db,
    keys,
    my_lines,
    their_lines,
    own,
    far_out,
    far_in,
    near_out,
    near_in,
    spread,
    send_out,
    arrived,
    switched,
    local_sem,
    db_sem,
    db_sems,
    keys_sem,
    query_sems,
    core_sems,
    far_sems,
    near_sems,
    owner_sems,
    across_sem,
):
    x, y, z, core = place()
    y_hi, y_lo = y // 2, lax.rem(y, 2)
    col = 2 * z + y_lo
    depth = keys_hbm.shape[1] // CHUNKS
    lane_groups = depth // 128

    def remote(src, dst, sems, index, target):
        return pltpu.make_async_remote_copy(
            src_ref=src,
            dst_ref=dst,
            send_sem=sems.at[(0, *index)],
            recv_sem=sems.at[(1, *index)],
            device_id=target,
            device_id_type=MESH,
        )

    partner = device(x, y, z, 1 - core)
    right, left = device(x + 1, y, z, core), device(x + 3, y, z, core)
    owners = [device(x, y + b // 4, z + b % 4, core) for b in range(16)]
    column_peers = []
    for dz, other in ((2, 1), (2, 0), (1, 1), (3, 1), (1, 0), (3, 0), (0, 1)):
        peer_y = 2 * y_hi + (1 - y_lo if other else y_lo)
        column_peers.append(device(x, peer_y, z + dz, core))
    across = device(x, y + 3 + 2 * y_lo, z, core)

    barrier = pltpu.get_barrier_semaphore()
    greeted = [*column_peers, across, partner, right, left]
    for target in greeted:
        pl.semaphore_signal(barrier, inc=1, device_id=target, device_id_type=MESH)
    pl.semaphore_wait(barrier, len(greeted))

    query_copies = []
    for i, target in enumerate(column_peers):
        copy = remote(query_hbm, gathered.at[col], query_sems, (i,), target)
        copy.start()
        query_copies.append(copy)

    slot_copy = pltpu.make_async_copy(slot_hbm, slots, local_sem.at[0])
    slot_copy.start()
    own_query = pltpu.make_async_copy(query_hbm, gathered.at[col], local_sem.at[1])
    own_query.start()
    db_swap = remote(db_hbm, db.at[1], db_sems, (), partner)
    db_swap.start()
    db_copy = pltpu.make_async_copy(db_hbm, db.at[0], db_sem)
    db_copy.start()
    keys_copy = pltpu.make_async_copy(keys_hbm, keys, keys_sem)
    keys_copy.start()

    slot_copy.wait()
    total = slots.shape[1]
    line = lax.broadcasted_iota(jnp.int32, (total, total), 0)
    place_at = lax.broadcasted_iota(jnp.int32, (total, total), 1)
    to_core = (line >> 7) + core & 1
    to_x = (line >> 5) + x & 3
    part = line >> 4 & 1
    to_y = (line >> 2) + y & 3
    to_z = line + z & 3
    owner_row = (to_x * 2 + (to_y >> 1)) * 2 + to_core
    owner_col = to_z * 2 + (to_y & 1)
    slot_of_line = (owner_row * 8 + owner_col) * 2 + part
    line_is_slot = jnp.where(slot_of_line == place_at, 1.0, 0.0).astype(BF16)
    client_at_slot = jnp.broadcast_to(slots[...], (total, total))
    client_is_slot = jnp.where(client_at_slot == line, 1.0, 0.0).astype(BF16)
    chooser = lax.dot_general(
        line_is_slot, client_is_slot, (((1,), (1,)), ((), ())), preferred_element_type=F32
    ).astype(BF16)

    own_query.wait()
    for copy in query_copies:
        copy.wait_recv()
    pl.semaphore_signal(across_sem, inc=1, device_id=across, device_id_type=MESH)
    entries = gathered[...].reshape(total, query_hbm.shape[1])
    chosen = jnp.dot(chooser, entries, preferred_element_type=F32).astype(BF16)
    half = total // 2

    sent = list(query_copies)
    far_copies, near_copies = {}, {}
    my_lines[...] = chosen[half:]
    lines_copy = remote(my_lines, their_lines, core_sems, (), partner)
    lines_copy.start()
    sent.append(lines_copy)
    db_copy.wait()
    db_swap.wait_recv()
    lines_copy.wait_recv()
    both_lines = jnp.concatenate([chosen[:half], their_lines[...]], axis=1)

    def multiply(k):
        for t in range(2):
            start = t * keys_hbm.shape[1] + k * depth
            block = db[:, :, start : start + depth]
            own[k, :, t * depth : (t + 1) * depth] = jnp.dot(
                both_lines,
                block.reshape(db.shape[0] * db.shape[1], depth),
                preferred_element_type=F32,
            )

    def start_near(k, side, lines):
        target = (right, left)[side]
        copy = remote(
            near_out.at[k, side, lines],
            near_in.at[k, side, lines],
            near_sems,
            (k, side, lines),
            target,
        )
        copy.start()
        near_copies[k, side, lines] = copy

    def send_far(k):
        for side in range(2):
            far_out[k, side] = own[k, pl.ds(64 + 16 * side, 16)].astype(BF16)
            copy = remote(
                far_out.at[k, side], far_in.at[k, side], far_sems, (k, side), (right, left)[side]
            )
            copy.start()
            far_copies[k, side] = copy

    def send_near(k):
        for side in range(2):
            near_out[k, side, 1 - side] = own[k, pl.ds((48, 96)[side], 16)].astype(BF16)
            start_near(k, side, 1 - side)

    def pass_on(k):
        for side in range(2):
            far_copies[k, side].wait_recv()
            lines = pl.ds((32, 112)[side], 16)
            near_out[k, side, side] = (own[k, lines] + far_in[k, side].astype(F32)).astype(BF16)
            start_near(k, side, side)

    far_first = sorted(range(16), key=lambda b: -min(b // 4, 4 - b // 4) - min(b % 4, 4 - b % 4))

    def to_owners(k):
        for part in range(2):
            for side in range(2):
                near_copies[k, side, part].wait_recv()
            lines = pl.ds(16 * part, 16)
            summed = (
                own[k, lines] + near_in[k, 0, part].astype(F32) + near_in[k, 1, part].astype(F32)
            )
            for t in range(2):
                for g in range(lane_groups):
                    lane = t * depth + g * 128
                    at = t * 2 * lane_groups + part * lane_groups + g
                    spread[pl.ds(at, 16, stride=4 * lane_groups), :] = summed[:, lane : lane + 128]
        send_out[k] = spread[...].astype(BF16).reshape(send_out.shape[1:])
        landing = arrived.at[k, y_hi, col]
        for b in far_first[:-1]:
            remote(send_out.at[k, b], landing, owner_sems, (k,), owners[b]).start()
        pltpu.make_async_copy(send_out.at[k, 0], landing, owner_sems.at[1, k]).start()

    totals = [None, None]

    def finish_sends(chunks):
        for k in chunks:
            block = send_out.at[k, pl.ds(1, 15)]
            pltpu.make_async_copy(block, block, owner_sems.at[0, k]).wait()


    def pack(k):
        pltpu.make_async_copy(arrived.at[k], arrived.at[k], owner_sems.at[1, k]).wait()
        both = arrived[k, 0].astype(F32) + arrived[k, 1].astype(F32)
        switched[...] = (both * factor).reshape(switched.shape)
        for part in range(2):
            pieces = [
                switched[pl.ds(part * lane_groups + g, 16, stride=2 * lane_groups), :]
                for g in range(lane_groups)
            ]
            tiles = jnp.concatenate(pieces, axis=1).astype(BF16)
            product = jnp.dot(tiles, keys[part, pl.ds(k * depth, depth)], preferred_element_type=F32)
            totals[part] = product if totals[part] is None else totals[part] + product

    multiply(0)
    send_far(0)
    multiply(1)
    send_far(1)
    multiply(2)
    send_far(2)
    multiply(3)
    send_far(3)
    send_near(0)
    pass_on(0)
    send_near(1)
    pass_on(1)
    send_near(2)
    pass_on(2)
    pl.semaphore_wait(across_sem, 1)
    to_owners(0)
    send_near(3)
    pass_on(3)
    to_owners(1)
    to_owners(2)
    to_owners(3)
    keys_copy.wait()
    sent.append(db_swap)
    for copies in (far_copies, near_copies):
        sent.extend(copies.values())
    for copy in sent:
        copy.wait_send()
    pack(0)
    pack(1)
    pack(2)
    finish_sends(range(0, 4))
    pack(3)
    for part in range(2):
        out_ref[part] = totals[part]


def shards(database, query, slot_map, keys):
    rows_axis = lax.axis_size("row")
    factor = float(database.shape[0] * rows_axis) ** (-0.5)
    total = slot_map.shape[0]
    rows, columns = database.shape
    tile, packs = keys.shape[1:]
    width = columns // CHUNKS
    half = total // 2
    dma = pltpu.SemaphoreType.DMA
    return pl.pallas_call(
        functools.partial(kernel, factor),
        out_shape=jax.ShapeDtypeStruct((2, 16, packs), F32),
        in_specs=[pl.BlockSpec(memory_space=pltpu.HBM)] * 4,
        out_specs=pl.BlockSpec(memory_space=pltpu.VMEM),
        scratch_shapes=[
            pltpu.VMEM((1, total), jnp.int32),
            pltpu.VMEM((8, total // 8, rows), BF16),
            pltpu.VMEM((2, rows, columns), BF16),
            pltpu.VMEM((2, tile, packs), BF16),
            pltpu.VMEM((half, rows), BF16),
            pltpu.VMEM((half, rows), BF16),
            pltpu.VMEM((CHUNKS, half, width), F32),
            pltpu.VMEM((CHUNKS, 2, 16, width), BF16),
            pltpu.VMEM((CHUNKS, 2, 16, width), BF16),
            pltpu.VMEM((CHUNKS, 2, 2, 16, width), BF16),
            pltpu.VMEM((CHUNKS, 2, 2, 16, width), BF16),
            pltpu.VMEM((tile // CHUNKS // 128 * 64, 128), F32),
            pltpu.VMEM((CHUNKS, 16, tile // CHUNKS // 32, 128), BF16),
            pltpu.VMEM((CHUNKS, 2, 8, tile // CHUNKS // 32, 128), BF16),
            pltpu.VMEM((tile // CHUNKS // 128 * 32, 128), F32),
            dma((2,)),
            dma(()),
            dma((2,)),
            dma(()),
            dma((2, 7)),
            dma((2,)),
            dma((2, CHUNKS, 2)),
            dma((2, CHUNKS, 2, 2)),
            dma((2, CHUNKS)),
            pltpu.SemaphoreType.REGULAR,
        ],
        compiler_params=pltpu.CompilerParams(
            collective_id=1, has_side_effects=True, vmem_limit_bytes=40 * 1024 * 1024
        ),
        name="answer_and_pack",
    )(*(pltpu.with_memory_space_constraint(a, pltpu.HBM) for a in (slot_map.reshape(1, total), query, database, keys)))


def solution(mesh):
    return jax.shard_map(
        shards,
        mesh=mesh,
        in_specs=(P("row", "col"), P("col", "row"), P(), P(("row", "col"), None, None)),
        out_specs=P(("row", "col"), None, None),
        check_vma=False,
    )
```

```python
import functools

import jax
import jax.numpy as jnp
from jax import lax
from jax.experimental import pallas as pl
from jax.experimental.pallas import tpu as pltpu
from jax.sharding import PartitionSpec as P

MESH = pl.DeviceIdType.MESH
CHUNKS = 4
F32 = jnp.float32
BF16 = jnp.bfloat16


def place():
    row, col = lax.axis_index("row"), lax.axis_index("col")
    x, y_hi, core = row // 4, lax.rem(row // 2, 2), lax.rem(row, 2)
    z, y_lo = col // 2, lax.rem(col, 2)
    return x, 2 * y_hi + y_lo, z, core


def device(x, y, z, core):
    x, y, z = lax.rem(x, 4), lax.rem(y, 4), lax.rem(z, 4)
    return ((2 * x + y // 2) * 2 + core, 2 * z + lax.rem(y, 2))


def kernel(
    factor,
    slot_hbm,
    query_hbm,
    db_hbm,
    keys_hbm,
    out_ref,
    slots,
    gathered,
    db,
    keys,
    my_lines,
    their_lines,
    own,
    far_out,
    far_in,
    near_out,
    near_in,
    spread,
    send_out,
    arrived,
    switched,
    local_sem,
    db_sem,
    db_sems,
    keys_sem,
    query_sems,
    core_sems,
    far_sems,
    near_sems,
    owner_sems,
    direct_out,
    direct_in,
    direct_sems,
    across_sem,
    plane_sem,
):
    x, y, z, core = place()
    y_hi, y_lo = y // 2, lax.rem(y, 2)
    col = 2 * z + y_lo
    depth = keys_hbm.shape[1] // CHUNKS
    lane_groups = depth // 128

    def remote(src, dst, sems, index, target):
        return pltpu.make_async_remote_copy(
            src_ref=src,
            dst_ref=dst,
            send_sem=sems.at[(0, *index)],
            recv_sem=sems.at[(1, *index)],
            device_id=target,
            device_id_type=MESH,
        )

    partner = device(x, y, z, 1 - core)
    right, left = device(x + 1, y, z, core), device(x + 3, y, z, core)
    owners = [device(x, y + b // 4, z + b % 4, core) for b in range(16)]
    column_peers = []
    for dz, other in ((2, 1), (2, 0), (1, 1), (3, 1), (1, 0), (3, 0), (0, 1)):
        peer_y = 2 * y_hi + (1 - y_lo if other else y_lo)
        column_peers.append(device(x, peer_y, z + dz, core))
    across = device(x, y + 3 + 2 * y_lo, z, core)

    barrier = pltpu.get_barrier_semaphore()
    greeted = [*column_peers, across, partner, right, left]
    for target in greeted:
        pl.semaphore_signal(barrier, inc=1, device_id=target, device_id_type=MESH)
    pl.semaphore_wait(barrier, len(greeted))

    query_copies = []
    for i, target in enumerate(column_peers):
        copy = remote(query_hbm, gathered.at[col], query_sems, (i,), target)
        copy.start()
        query_copies.append(copy)

    slot_copy = pltpu.make_async_copy(slot_hbm, slots, local_sem.at[0])
    slot_copy.start()
    own_query = pltpu.make_async_copy(query_hbm, gathered.at[col], local_sem.at[1])
    own_query.start()
    db_swap = remote(db_hbm, db.at[1], db_sems, (), partner)
    db_swap.start()
    db_copy = pltpu.make_async_copy(db_hbm, db.at[0], db_sem)
    db_copy.start()
    keys_copy = pltpu.make_async_copy(keys_hbm, keys, keys_sem)
    keys_copy.start()

    slot_copy.wait()
    total = slots.shape[1]
    line = lax.broadcasted_iota(jnp.int32, (total, total), 0)
    place_at = lax.broadcasted_iota(jnp.int32, (total, total), 1)
    to_core = (line >> 7) + core & 1
    to_x = (line >> 5) + x & 3
    part = line >> 4 & 1
    to_y = (line >> 2) + y & 3
    to_z = line + z & 3
    owner_row = (to_x * 2 + (to_y >> 1)) * 2 + to_core
    owner_col = to_z * 2 + (to_y & 1)
    slot_of_line = (owner_row * 8 + owner_col) * 2 + part
    line_is_slot = jnp.where(slot_of_line == place_at, 1.0, 0.0).astype(BF16)
    client_at_slot = jnp.broadcast_to(slots[...], (total, total))
    client_is_slot = jnp.where(client_at_slot == line, 1.0, 0.0).astype(BF16)
    chooser = lax.dot_general(
        line_is_slot, client_is_slot, (((1,), (1,)), ((), ())), preferred_element_type=F32
    ).astype(BF16)

    own_query.wait()
    for copy in query_copies:
        copy.wait_recv()
    pl.semaphore_signal(across_sem, inc=1, device_id=across, device_id_type=MESH)
    entries = gathered[...].reshape(total, query_hbm.shape[1])
    chosen = jnp.dot(chooser, entries, preferred_element_type=F32).astype(BF16)
    half = total // 2

    sent = list(query_copies)
    far_copies, near_copies = {}, {}
    my_lines[...] = chosen[half:]
    lines_copy = remote(my_lines, their_lines, core_sems, (), partner)
    lines_copy.start()
    sent.append(lines_copy)
    db_copy.wait()
    db_swap.wait_recv()
    lines_copy.wait_recv()
    both_lines = jnp.concatenate([chosen[:half], their_lines[...]], axis=1)

    def multiply(k):
        for t in range(2):
            start = t * keys_hbm.shape[1] + k * depth
            block = db[:, :, start : start + depth]
            own[k, :, t * depth : (t + 1) * depth] = jnp.dot(
                both_lines,
                block.reshape(db.shape[0] * db.shape[1], depth),
                preferred_element_type=F32,
            )

    def start_near(k, side, lines):
        target = (right, left)[side]
        copy = remote(
            near_out.at[k, side, lines],
            near_in.at[k, side, lines],
            near_sems,
            (k, side, lines),
            target,
        )
        copy.start()
        near_copies[k, side, lines] = copy

    def send_far(k):
        for side in range(2):
            far_out[k, side] = own[k, pl.ds(64 + 16 * side, 16)].astype(BF16)
            copy = remote(
                far_out.at[k, side], far_in.at[k, side], far_sems, (k, side), (right, left)[side]
            )
            copy.start()
            far_copies[k, side] = copy

    def send_near(k):
        for side in range(2):
            near_out[k, side, 1 - side] = own[k, pl.ds((48, 96)[side], 16)].astype(BF16)
            start_near(k, side, 1 - side)

    def pass_on(k):
        for side in range(2):
            far_copies[k, side].wait_recv()
            lines = pl.ds((32, 112)[side], 16)
            near_out[k, side, side] = (own[k, lines] + far_in[k, side].astype(F32)).astype(BF16)
            start_near(k, side, side)

    far_first = sorted(range(16), key=lambda b: -min(b // 4, 4 - b // 4) - min(b % 4, 4 - b % 4))

    def to_owners(k):
        for part in range(2):
            for side in range(2):
                near_copies[k, side, part].wait_recv()
            lines = pl.ds(16 * part, 16)
            summed = (
                own[k, lines] + near_in[k, 0, part].astype(F32) + near_in[k, 1, part].astype(F32)
            )
            for t in range(2):
                for g in range(lane_groups):
                    lane = t * depth + g * 128
                    at = t * 2 * lane_groups + part * lane_groups + g
                    spread[pl.ds(at, 16, stride=4 * lane_groups), :] = summed[:, lane : lane + 128]
        send_out[k] = spread[...].astype(BF16).reshape(send_out.shape[1:])
        landing = arrived.at[k, y_hi, col]
        for b in far_first[:-1]:
            remote(send_out.at[k, b], landing, owner_sems, (k,), owners[b]).start()
        pltpu.make_async_copy(send_out.at[k, 0], landing, owner_sems.at[1, k]).start()

    def direct(origins):
        for origin in origins:
            if origin:
                side = origin - 1
                copy = far_copies[CHUNKS - 1, side]
                copy.wait_recv()
            for part in range(2):
                first = (0, 32, 96)[origin] + 16 * part
                summed = own[CHUNKS - 1, pl.ds(first, 16)]
                if origin and part == side:
                    summed = summed + far_in[CHUNKS - 1, side].astype(F32)
                for t in range(2):
                    for g in range(lane_groups):
                        lane = t * depth + g * 128
                        at = t * 2 * lane_groups + part * lane_groups + g
                        spread[pl.ds(at, 16, stride=4 * lane_groups), :] = summed[
                            :, lane : lane + 128
                        ]
            direct_out[origin] = spread[...].astype(BF16).reshape(direct_out.shape[1:])
        for b in far_first:
            for origin in origins:
                landing = direct_in.at[origin, y_hi, col]
                if b or origin:
                    target = device(x + (0, 1, 3)[origin], y + b // 4, z + b % 4, core)
                    remote(direct_out.at[origin, b], landing, direct_sems, (origin,), target).start()
                else:
                    pltpu.make_async_copy(
                        direct_out.at[0, 0], landing, direct_sems.at[1, 0]
                    ).start()

    totals = [None, None]

    def finish_sends(chunks):
        for k in chunks:
            block = send_out.at[k, pl.ds(1, 15)]
            pltpu.make_async_copy(block, block, owner_sems.at[0, k]).wait()


    def pack(k):
        if k < CHUNKS - 1:
            pltpu.make_async_copy(arrived.at[k], arrived.at[k], owner_sems.at[1, k]).wait()
            both = arrived[k, 0].astype(F32) + arrived[k, 1].astype(F32)
        else:
            both = None
            for origin in (0, 1, 2):
                block = direct_in.at[origin]
                pltpu.make_async_copy(block, block, direct_sems.at[1, origin]).wait()
                pair = direct_in[origin, 0].astype(F32) + direct_in[origin, 1].astype(F32)
                both = pair if both is None else both + pair
        switched[...] = (both * factor).reshape(switched.shape)
        for part in range(2):
            pieces = [
                switched[pl.ds(part * lane_groups + g, 16, stride=2 * lane_groups), :]
                for g in range(lane_groups)
            ]
            tiles = jnp.concatenate(pieces, axis=1).astype(BF16)
            product = jnp.dot(tiles, keys[part, pl.ds(k * depth, depth)], preferred_element_type=F32)
            totals[part] = product if totals[part] is None else totals[part] + product

    multiply(3)
    send_far(3)
    multiply(0)
    send_far(0)
    multiply(1)
    send_far(1)
    multiply(2)
    send_far(2)
    send_near(0)
    send_near(1)
    pass_on(0)
    pl.semaphore_wait(across_sem, 1)
    for target in (right, left):
        pl.semaphore_signal(plane_sem, inc=1, device_id=target, device_id_type=MESH)
    send_near(2)
    pass_on(1)
    pass_on(2)
    pl.semaphore_wait(plane_sem, 2)
    direct((0,))
    direct((1, 2))
    to_owners(0)
    to_owners(1)
    to_owners(2)
    keys_copy.wait()
    sent.append(db_swap)
    for copies in (far_copies, near_copies):
        sent.extend(copies.values())
    for copy in sent:
        copy.wait_send()
    pack(0)
    pack(1)
    pack(2)
    finish_sends(range(CHUNKS - 1))
    for origin in range(3):
        block = direct_out.at[origin] if origin else direct_out.at[0, pl.ds(1, 15)]
        pltpu.make_async_copy(block, block, direct_sems.at[0, origin]).wait()
    pack(3)
    for part in range(2):
        out_ref[part] = totals[part]


def shards(database, query, slot_map, keys):
    rows_axis = lax.axis_size("row")
    factor = float(database.shape[0] * rows_axis) ** (-0.5)
    total = slot_map.shape[0]
    rows, columns = database.shape
    tile, packs = keys.shape[1:]
    width = columns // CHUNKS
    half = total // 2
    dma = pltpu.SemaphoreType.DMA
    return pl.pallas_call(
        functools.partial(kernel, factor),
        out_shape=jax.ShapeDtypeStruct((2, 16, packs), F32),
        in_specs=[pl.BlockSpec(memory_space=pltpu.HBM)] * 4,
        out_specs=pl.BlockSpec(memory_space=pltpu.VMEM),
        scratch_shapes=[
            pltpu.VMEM((1, total), jnp.int32),
            pltpu.VMEM((8, total // 8, rows), BF16),
            pltpu.VMEM((2, rows, columns), BF16),
            pltpu.VMEM((2, tile, packs), BF16),
            pltpu.VMEM((half, rows), BF16),
            pltpu.VMEM((half, rows), BF16),
            pltpu.VMEM((CHUNKS, half, width), F32),
            pltpu.VMEM((CHUNKS, 2, 16, width), BF16),
            pltpu.VMEM((CHUNKS, 2, 16, width), BF16),
            pltpu.VMEM((CHUNKS - 1, 2, 2, 16, width), BF16),
            pltpu.VMEM((CHUNKS - 1, 2, 2, 16, width), BF16),
            pltpu.VMEM((tile // CHUNKS // 128 * 64, 128), F32),
            pltpu.VMEM((CHUNKS - 1, 16, tile // CHUNKS // 32, 128), BF16),
            pltpu.VMEM((CHUNKS - 1, 2, 8, tile // CHUNKS // 32, 128), BF16),
            pltpu.VMEM((tile // CHUNKS // 128 * 32, 128), F32),
            dma((2,)),
            dma(()),
            dma((2,)),
            dma(()),
            dma((2, 7)),
            dma((2,)),
            dma((2, CHUNKS, 2)),
            dma((2, CHUNKS - 1, 2, 2)),
            dma((2, CHUNKS - 1)),
            pltpu.VMEM((3, 16, tile // CHUNKS // 32, 128), BF16),
            pltpu.VMEM((3, 2, 8, tile // CHUNKS // 32, 128), BF16),
            dma((2, 3)),
            pltpu.SemaphoreType.REGULAR,
            pltpu.SemaphoreType.REGULAR,
        ],
        compiler_params=pltpu.CompilerParams(
            collective_id=1, has_side_effects=True, vmem_limit_bytes=40 * 1024 * 1024
        ),
        name="answer_and_pack",
    )(*(pltpu.with_memory_space_constraint(a, pltpu.HBM) for a in (slot_map.reshape(1, total), query, database, keys)))


def solution(mesh):
    return jax.shard_map(
        shards,
        mesh=mesh,
        in_specs=(P("row", "col"), P("col", "row"), P(), P(("row", "col"), None, None)),
        out_specs=P(("row", "col"), None, None),
        check_vma=False,
    )
```

```python
import functools

import jax
import jax.numpy as jnp
from jax import lax
from jax.experimental import pallas as pl
from jax.experimental.pallas import tpu as pltpu
from jax.sharding import PartitionSpec as P

MESH = pl.DeviceIdType.MESH
CHUNKS = 4
STAGED = 3
F32 = jnp.float32
BF16 = jnp.bfloat16


def place():
    row, col = lax.axis_index("row"), lax.axis_index("col")
    x, y_hi, core = row // 4, lax.rem(row // 2, 2), lax.rem(row, 2)
    z, y_lo = col // 2, lax.rem(col, 2)
    return x, 2 * y_hi + y_lo, z, core


def device(x, y, z, core):
    x, y, z = lax.rem(x, 4), lax.rem(y, 4), lax.rem(z, 4)
    return ((2 * x + y // 2) * 2 + core, 2 * z + lax.rem(y, 2))


def kernel(
    factor,
    slot_hbm,
    query_hbm,
    db_hbm,
    keys_hbm,
    out_ref,
    slots,
    gathered,
    db,
    keys,
    my_lines,
    their_lines,
    own,
    far_out,
    far_in,
    near_out,
    near_in,
    spread,
    send_out,
    arrived,
    switched,
    local_sem,
    db_sem,
    db_sems,
    keys_sem,
    query_sems,
    core_sems,
    far_sems,
    near_sems,
    owner_sems,
    direct_out,
    direct_in,
    direct_sems,
    across_sem,
    plane_sem,
):
    x, y, z, core = place()
    y_hi, y_lo = y // 2, lax.rem(y, 2)
    col = 2 * z + y_lo
    depth = keys_hbm.shape[1] // CHUNKS
    lane_groups = depth // 128

    def remote(src, dst, sems, index, target):
        return pltpu.make_async_remote_copy(
            src_ref=src,
            dst_ref=dst,
            send_sem=sems.at[(0, *index)],
            recv_sem=sems.at[(1, *index)],
            device_id=target,
            device_id_type=MESH,
        )

    partner = device(x, y, z, 1 - core)
    right, left = device(x + 1, y, z, core), device(x + 3, y, z, core)
    owners = [device(x, y + b // 4, z + b % 4, core) for b in range(16)]
    column_peers = []
    for dz, other in ((2, 1), (2, 0), (1, 1), (3, 1), (1, 0), (3, 0), (0, 1)):
        peer_y = 2 * y_hi + (1 - y_lo if other else y_lo)
        column_peers.append(device(x, peer_y, z + dz, core))
    across = device(x, y + 3 + 2 * y_lo, z, core)

    barrier = pltpu.get_barrier_semaphore()
    greeted = [*column_peers, across, partner, right, left]
    for target in greeted:
        pl.semaphore_signal(barrier, inc=1, device_id=target, device_id_type=MESH)
    pl.semaphore_wait(barrier, len(greeted))

    query_copies = []
    for i, target in enumerate(column_peers):
        copy = remote(query_hbm, gathered.at[col], query_sems, (i,), target)
        copy.start()
        query_copies.append(copy)

    slot_copy = pltpu.make_async_copy(slot_hbm, slots, local_sem.at[0])
    slot_copy.start()
    own_query = pltpu.make_async_copy(query_hbm, gathered.at[col], local_sem.at[1])
    own_query.start()
    db_swap = remote(db_hbm, db.at[1], db_sems, (), partner)
    db_swap.start()
    db_copy = pltpu.make_async_copy(db_hbm, db.at[0], db_sem)
    db_copy.start()
    keys_copy = pltpu.make_async_copy(keys_hbm, keys, keys_sem)
    keys_copy.start()

    slot_copy.wait()
    total = slots.shape[1]
    line = lax.broadcasted_iota(jnp.int32, (total, total), 0)
    place_at = lax.broadcasted_iota(jnp.int32, (total, total), 1)
    to_core = (line >> 7) + core & 1
    to_x = (line >> 5) + x & 3
    part = line >> 4 & 1
    to_y = (line >> 2) + y & 3
    to_z = line + z & 3
    owner_row = (to_x * 2 + (to_y >> 1)) * 2 + to_core
    owner_col = to_z * 2 + (to_y & 1)
    slot_of_line = (owner_row * 8 + owner_col) * 2 + part
    line_is_slot = jnp.where(slot_of_line == place_at, 1.0, 0.0).astype(BF16)
    client_at_slot = jnp.broadcast_to(slots[...], (total, total))
    client_is_slot = jnp.where(client_at_slot == line, 1.0, 0.0).astype(BF16)
    chooser = lax.dot_general(
        line_is_slot, client_is_slot, (((1,), (1,)), ((), ())), preferred_element_type=F32
    ).astype(BF16)

    own_query.wait()
    for copy in query_copies:
        copy.wait_recv()
    pl.semaphore_signal(across_sem, inc=1, device_id=across, device_id_type=MESH)
    entries = gathered[...].reshape(total, query_hbm.shape[1])
    chosen = jnp.dot(chooser, entries, preferred_element_type=F32).astype(BF16)
    half = total // 2

    sent = list(query_copies)
    far_copies, near_copies = {}, {}
    my_lines[...] = chosen[half:]
    lines_copy = remote(my_lines, their_lines, core_sems, (), partner)
    lines_copy.start()
    sent.append(lines_copy)
    db_copy.wait()
    db_swap.wait_recv()
    lines_copy.wait_recv()
    both_lines = jnp.concatenate([chosen[:half], their_lines[...]], axis=1)

    def multiply(k):
        for t in range(2):
            start = t * keys_hbm.shape[1] + k * depth
            block = db[:, :, start : start + depth]
            own[k, :, t * depth : (t + 1) * depth] = jnp.dot(
                both_lines,
                block.reshape(db.shape[0] * db.shape[1], depth),
                preferred_element_type=F32,
            )

    def start_near(k, side, lines):
        target = (right, left)[side]
        copy = remote(
            near_out.at[k, side, lines],
            near_in.at[k, side, lines],
            near_sems,
            (k, side, lines),
            target,
        )
        copy.start()
        near_copies[k, side, lines] = copy

    def send_far(k):
        for side in range(2):
            far_out[k, side] = own[k, pl.ds(64 + 16 * side, 16)].astype(BF16)
            copy = remote(
                far_out.at[k, side], far_in.at[k, side], far_sems, (k, side), (right, left)[side]
            )
            copy.start()
            far_copies[k, side] = copy

    def send_near(k):
        for side in range(2):
            near_out[k, side, 1 - side] = own[k, pl.ds((48, 96)[side], 16)].astype(BF16)
            start_near(k, side, 1 - side)

    def pass_on(k):
        for side in range(2):
            far_copies[k, side].wait_recv()
            lines = pl.ds((32, 112)[side], 16)
            near_out[k, side, side] = (own[k, lines] + far_in[k, side].astype(F32)).astype(BF16)
            start_near(k, side, side)

    far_first = sorted(range(16), key=lambda b: -min(b // 4, 4 - b // 4) - min(b % 4, 4 - b % 4))

    def to_owners(k):
        for part in range(2):
            for side in range(2):
                near_copies[k, side, part].wait_recv()
            lines = pl.ds(16 * part, 16)
            summed = (
                own[k, lines] + near_in[k, 0, part].astype(F32) + near_in[k, 1, part].astype(F32)
            )
            for t in range(2):
                for g in range(lane_groups):
                    lane = t * depth + g * 128
                    at = t * 2 * lane_groups + part * lane_groups + g
                    spread[pl.ds(at, 16, stride=4 * lane_groups), :] = summed[:, lane : lane + 128]
        send_out[k] = spread[...].astype(BF16).reshape(send_out.shape[1:])
        landing = arrived.at[k, y_hi, col]
        for b in far_first[:-1]:
            remote(send_out.at[k, b], landing, owner_sems, (k,), owners[b]).start()
        pltpu.make_async_copy(send_out.at[k, 0], landing, owner_sems.at[1, k]).start()

    def direct(origins):
        for origin in origins:
            for k in range(STAGED, CHUNKS):
                side = origin - 1
                if origin:
                    far_copies[k, side].wait_recv()
                for part in range(2):
                    summed = own[k, pl.ds((0, 32, 96)[origin] + 16 * part, 16)]
                    if origin and part == side:
                        summed = summed + far_in[k, side].astype(F32)
                    for t in range(2):
                        for g in range(lane_groups):
                            lane = t * depth + g * 128
                            at = t * 2 * lane_groups + part * lane_groups + g
                            spread[pl.ds(at, 16, stride=4 * lane_groups), :] = summed[
                                :, lane : lane + 128
                            ]
                direct_out[origin, :, k - STAGED] = spread[...].astype(BF16).reshape(
                    16, *direct_out.shape[3:]
                )
        for b in far_first:
            for origin in origins:
                landing = direct_in.at[origin, y_hi, col]
                if b or origin:
                    target = device(x + (0, 1, 3)[origin], y + b // 4, z + b % 4, core)
                    remote(direct_out.at[origin, b], landing, direct_sems, (origin,), target).start()
                else:
                    pltpu.make_async_copy(
                        direct_out.at[0, 0], landing, direct_sems.at[1, 0]
                    ).start()

    totals = [None, None]

    def finish_sends(chunks):
        for k in chunks:
            block = send_out.at[k, pl.ds(1, 15)]
            pltpu.make_async_copy(block, block, owner_sems.at[0, k]).wait()


    def pack(k):
        if k < STAGED:
            pltpu.make_async_copy(arrived.at[k], arrived.at[k], owner_sems.at[1, k]).wait()
            both = arrived[k, 0].astype(F32) + arrived[k, 1].astype(F32)
        else:
            both = None
            for origin in (0, 1, 2):
                block = direct_in.at[origin]
                if k == STAGED:
                    pltpu.make_async_copy(block, block, direct_sems.at[1, origin]).wait()
                pair = direct_in[origin, 0, :, k - STAGED].astype(F32)
                pair = pair + direct_in[origin, 1, :, k - STAGED].astype(F32)
                both = pair if both is None else both + pair
        switched[...] = (both * factor).reshape(switched.shape)
        for part in range(2):
            pieces = [
                switched[pl.ds(part * lane_groups + g, 16, stride=2 * lane_groups), :]
                for g in range(lane_groups)
            ]
            tiles = jnp.concatenate(pieces, axis=1).astype(BF16)
            product = jnp.dot(tiles, keys[part, pl.ds(k * depth, depth)], preferred_element_type=F32)
            totals[part] = product if totals[part] is None else totals[part] + product

    multiply(3)
    send_far(3)
    multiply(0)
    send_far(0)
    multiply(1)
    send_far(1)
    multiply(2)
    send_far(2)
    send_near(0)
    pass_on(0)
    send_near(1)
    pl.semaphore_wait(across_sem, 1)
    for target in (right, left):
        pl.semaphore_signal(plane_sem, inc=1, device_id=target, device_id_type=MESH)
    pass_on(1)
    send_near(2)
    pass_on(2)
    pl.semaphore_wait(plane_sem, 2)
    direct((0,))
    direct((1, 2))
    to_owners(0)
    to_owners(1)
    to_owners(2)
    keys_copy.wait()
    sent.append(db_swap)
    for copies in (far_copies, near_copies):
        sent.extend(copies.values())
    for copy in sent:
        copy.wait_send()
    pack(0)
    pack(1)
    pack(2)
    finish_sends(range(STAGED))
    for origin in range(3):
        block = direct_out.at[origin] if origin else direct_out.at[0, pl.ds(1, 15)]
        pltpu.make_async_copy(block, block, direct_sems.at[0, origin]).wait()
    pack(3)
    for part in range(2):
        out_ref[part] = totals[part]


def shards(database, query, slot_map, keys):
    rows_axis = lax.axis_size("row")
    factor = float(database.shape[0] * rows_axis) ** (-0.5)
    total = slot_map.shape[0]
    rows, columns = database.shape
    tile, packs = keys.shape[1:]
    width = columns // CHUNKS
    half = total // 2
    dma = pltpu.SemaphoreType.DMA
    return pl.pallas_call(
        functools.partial(kernel, factor),
        out_shape=jax.ShapeDtypeStruct((2, 16, packs), F32),
        in_specs=[pl.BlockSpec(memory_space=pltpu.HBM)] * 4,
        out_specs=pl.BlockSpec(memory_space=pltpu.VMEM),
        scratch_shapes=[
            pltpu.VMEM((1, total), jnp.int32),
            pltpu.VMEM((8, total // 8, rows), BF16),
            pltpu.VMEM((2, rows, columns), BF16),
            pltpu.VMEM((2, tile, packs), BF16),
            pltpu.VMEM((half, rows), BF16),
            pltpu.VMEM((half, rows), BF16),
            pltpu.VMEM((CHUNKS, half, width), F32),
            pltpu.VMEM((CHUNKS, 2, 16, width), BF16),
            pltpu.VMEM((CHUNKS, 2, 16, width), BF16),
            pltpu.VMEM((STAGED, 2, 2, 16, width), BF16),
            pltpu.VMEM((STAGED, 2, 2, 16, width), BF16),
            pltpu.VMEM((tile // CHUNKS // 128 * 64, 128), F32),
            pltpu.VMEM((STAGED, 16, tile // CHUNKS // 32, 128), BF16),
            pltpu.VMEM((STAGED, 2, 8, tile // CHUNKS // 32, 128), BF16),
            pltpu.VMEM((tile // CHUNKS // 128 * 32, 128), F32),
            dma((2,)),
            dma(()),
            dma((2,)),
            dma(()),
            dma((2, 7)),
            dma((2,)),
            dma((2, CHUNKS, 2)),
            dma((2, STAGED, 2, 2)),
            dma((2, STAGED)),
            pltpu.VMEM((3, 16, CHUNKS - STAGED, tile // CHUNKS // 32, 128), BF16),
            pltpu.VMEM((3, 2, 8, CHUNKS - STAGED, tile // CHUNKS // 32, 128), BF16),
            dma((2, 3)),
            pltpu.SemaphoreType.REGULAR,
            pltpu.SemaphoreType.REGULAR,
        ],
        compiler_params=pltpu.CompilerParams(
            collective_id=1, has_side_effects=True, vmem_limit_bytes=40 * 1024 * 1024
        ),
        name="answer_and_pack",
    )(*(pltpu.with_memory_space_constraint(a, pltpu.HBM) for a in (slot_map.reshape(1, total), query, database, keys)))


def solution(mesh):
    return jax.shard_map(
        shards,
        mesh=mesh,
        in_specs=(P("row", "col"), P("col", "row"), P(), P(("row", "col"), None, None)),
        out_specs=P(("row", "col"), None, None),
        check_vma=False,
    )
```

```python
import functools

import jax
import jax.numpy as jnp
from jax import lax
from jax.experimental import pallas as pl
from jax.experimental.pallas import tpu as pltpu
from jax.sharding import PartitionSpec as P

MESH = pl.DeviceIdType.MESH
CHUNKS = 4
STAGED = 3
F32 = jnp.float32
BF16 = jnp.bfloat16


def place():
    row, col = lax.axis_index("row"), lax.axis_index("col")
    x, y_hi, core = row // 4, lax.rem(row // 2, 2), lax.rem(row, 2)
    z, y_lo = col // 2, lax.rem(col, 2)
    return x, 2 * y_hi + y_lo, z, core


def device(x, y, z, core):
    x, y, z = lax.rem(x, 4), lax.rem(y, 4), lax.rem(z, 4)
    return ((2 * x + y // 2) * 2 + core, 2 * z + lax.rem(y, 2))


def kernel(
    factor,
    slot_hbm,
    query_hbm,
    db_hbm,
    keys_hbm,
    out_ref,
    slots,
    gathered,
    db,
    keys,
    my_lines,
    their_lines,
    own,
    far_out,
    far_in,
    near_out,
    near_in,
    spread,
    send_out,
    arrived,
    switched,
    local_sem,
    db_sem,
    db_sems,
    keys_sem,
    query_sems,
    core_sems,
    far_sems,
    near_sems,
    owner_sems,
    direct_out,
    direct_in,
    direct_sems,
    across_sem,
    plane_sem,
):
    x, y, z, core = place()
    y_hi, y_lo = y // 2, lax.rem(y, 2)
    col = 2 * z + y_lo
    depth = keys_hbm.shape[1] // CHUNKS
    lane_groups = depth // 128

    def remote(src, dst, sems, index, target):
        return pltpu.make_async_remote_copy(
            src_ref=src,
            dst_ref=dst,
            send_sem=sems.at[(0, *index)],
            recv_sem=sems.at[(1, *index)],
            device_id=target,
            device_id_type=MESH,
        )

    partner = device(x, y, z, 1 - core)
    right, left = device(x + 1, y, z, core), device(x + 3, y, z, core)
    owners = [device(x, y + b // 4, z + b % 4, core) for b in range(16)]
    column_peers = []
    for dz, other in ((2, 1), (2, 0), (1, 1), (3, 1), (1, 0), (3, 0), (0, 1)):
        peer_y = 2 * y_hi + (1 - y_lo if other else y_lo)
        column_peers.append(device(x, peer_y, z + dz, core))
    across = device(x, y + 3 + 2 * y_lo, z, core)

    barrier = pltpu.get_barrier_semaphore()
    greeted = [*column_peers, across, partner, right, left]
    for target in greeted:
        pl.semaphore_signal(barrier, inc=1, device_id=target, device_id_type=MESH)
    pl.semaphore_wait(barrier, len(greeted))

    query_copies = []
    for i, target in enumerate(column_peers):
        copy = remote(query_hbm, gathered.at[col], query_sems, (i,), target)
        copy.start()
        query_copies.append(copy)

    slot_copy = pltpu.make_async_copy(slot_hbm, slots, local_sem.at[0])
    slot_copy.start()
    own_query = pltpu.make_async_copy(query_hbm, gathered.at[col], local_sem.at[1])
    own_query.start()
    db_swap = remote(db_hbm, db.at[1], db_sems, (), partner)
    db_swap.start()
    db_copy = pltpu.make_async_copy(db_hbm, db.at[0], db_sem)
    db_copy.start()
    keys_copy = pltpu.make_async_copy(keys_hbm, keys, keys_sem)
    keys_copy.start()

    slot_copy.wait()
    total = slots.shape[1]
    line = lax.broadcasted_iota(jnp.int32, (total, total), 0)
    place_at = lax.broadcasted_iota(jnp.int32, (total, total), 1)
    to_core = (line >> 7) + core & 1
    to_x = (line >> 5) + x & 3
    part = line >> 4 & 1
    to_y = (line >> 2) + y & 3
    to_z = line + z & 3
    owner_row = (to_x * 2 + (to_y >> 1)) * 2 + to_core
    owner_col = to_z * 2 + (to_y & 1)
    slot_of_line = (owner_row * 8 + owner_col) * 2 + part
    line_is_slot = jnp.where(slot_of_line == place_at, 1.0, 0.0).astype(BF16)
    client_at_slot = jnp.broadcast_to(slots[...], (total, total))
    client_is_slot = jnp.where(client_at_slot == line, 1.0, 0.0).astype(BF16)
    chooser = lax.dot_general(
        line_is_slot, client_is_slot, (((1,), (1,)), ((), ())), preferred_element_type=F32
    ).astype(BF16)

    own_query.wait()
    for copy in query_copies:
        copy.wait_recv()
    entries = gathered[...].reshape(total, query_hbm.shape[1])
    half = total // 2

    def choose(lines):
        return jnp.dot(lines, entries, preferred_element_type=F32).astype(BF16)

    sent = list(query_copies)
    far_copies, near_copies = {}, {}
    my_lines[...] = choose(chooser[half:])
    lines_copy = remote(my_lines, their_lines, core_sems, (), partner)
    lines_copy.start()
    pl.semaphore_signal(across_sem, inc=1, device_id=across, device_id_type=MESH)
    own_lines = choose(chooser[:half])
    sent.append(lines_copy)
    db_copy.wait()
    db_swap.wait_recv()
    lines_copy.wait_recv()
    both_lines = jnp.concatenate([own_lines, their_lines[...]], axis=1)

    def multiply(k):
        for t in range(2):
            start = t * keys_hbm.shape[1] + k * depth
            block = db[:, :, start : start + depth]
            own[k, :, t * depth : (t + 1) * depth] = jnp.dot(
                both_lines,
                block.reshape(db.shape[0] * db.shape[1], depth),
                preferred_element_type=F32,
            )

    def start_near(k, side, lines):
        target = (right, left)[side]
        copy = remote(
            near_out.at[k, side, lines],
            near_in.at[k, side, lines],
            near_sems,
            (k, side, lines),
            target,
        )
        copy.start()
        near_copies[k, side, lines] = copy

    def send_far(k):
        for side in range(2):
            far_out[k, side] = own[k, pl.ds(64 + 16 * side, 16)].astype(BF16)
            copy = remote(
                far_out.at[k, side], far_in.at[k, side], far_sems, (k, side), (right, left)[side]
            )
            copy.start()
            far_copies[k, side] = copy

    def send_near(k):
        for side in range(2):
            near_out[k, side, 1 - side] = own[k, pl.ds((48, 96)[side], 16)].astype(BF16)
            start_near(k, side, 1 - side)

    def pass_on(k):
        for side in range(2):
            far_copies[k, side].wait_recv()
            lines = pl.ds((32, 112)[side], 16)
            near_out[k, side, side] = (own[k, lines] + far_in[k, side].astype(F32)).astype(BF16)
            start_near(k, side, side)

    far_first = sorted(range(16), key=lambda b: -min(b // 4, 4 - b // 4) - min(b % 4, 4 - b % 4))

    def to_owners(k):
        for part in range(2):
            for side in range(2):
                near_copies[k, side, part].wait_recv()
            lines = pl.ds(16 * part, 16)
            summed = (
                own[k, lines] + near_in[k, 0, part].astype(F32) + near_in[k, 1, part].astype(F32)
            )
            for t in range(2):
                for g in range(lane_groups):
                    lane = t * depth + g * 128
                    at = t * 2 * lane_groups + part * lane_groups + g
                    spread[pl.ds(at, 16, stride=4 * lane_groups), :] = summed[:, lane : lane + 128]
        send_out[k] = spread[...].astype(BF16).reshape(send_out.shape[1:])
        landing = arrived.at[k, y_hi, col]
        for b in far_first[:-1]:
            remote(send_out.at[k, b], landing, owner_sems, (k,), owners[b]).start()
        pltpu.make_async_copy(send_out.at[k, 0], landing, owner_sems.at[1, k]).start()

    def direct(origins):
        for origin in origins:
            for k in range(STAGED, CHUNKS):
                side = origin - 1
                if origin:
                    far_copies[k, side].wait_recv()
                for part in range(2):
                    summed = own[k, pl.ds((0, 32, 96)[origin] + 16 * part, 16)]
                    if origin and part == side:
                        summed = summed + far_in[k, side].astype(F32)
                    for t in range(2):
                        for g in range(lane_groups):
                            lane = t * depth + g * 128
                            at = t * 2 * lane_groups + part * lane_groups + g
                            spread[pl.ds(at, 16, stride=4 * lane_groups), :] = summed[
                                :, lane : lane + 128
                            ]
                direct_out[origin, :, k - STAGED] = spread[...].astype(BF16).reshape(
                    16, *direct_out.shape[3:]
                )
        for b in far_first:
            for origin in origins:
                landing = direct_in.at[origin, y_hi, col]
                if b or origin:
                    target = device(x + (0, 1, 3)[origin], y + b // 4, z + b % 4, core)
                    remote(direct_out.at[origin, b], landing, direct_sems, (origin,), target).start()
                else:
                    pltpu.make_async_copy(
                        direct_out.at[0, 0], landing, direct_sems.at[1, 0]
                    ).start()

    totals = [None, None]

    def finish_sends(chunks):
        for k in chunks:
            block = send_out.at[k, pl.ds(1, 15)]
            pltpu.make_async_copy(block, block, owner_sems.at[0, k]).wait()


    def pack(k):
        if k < STAGED:
            pltpu.make_async_copy(arrived.at[k], arrived.at[k], owner_sems.at[1, k]).wait()
            both = arrived[k, 0].astype(F32) + arrived[k, 1].astype(F32)
        else:
            both = None
            for origin in (0, 1, 2):
                block = direct_in.at[origin]
                if k == STAGED:
                    pltpu.make_async_copy(block, block, direct_sems.at[1, origin]).wait()
                pair = direct_in[origin, 0, :, k - STAGED].astype(F32)
                pair = pair + direct_in[origin, 1, :, k - STAGED].astype(F32)
                both = pair if both is None else both + pair
        switched[...] = (both * factor).reshape(switched.shape)
        for part in range(2):
            pieces = [
                switched[pl.ds(part * lane_groups + g, 16, stride=2 * lane_groups), :]
                for g in range(lane_groups)
            ]
            tiles = jnp.concatenate(pieces, axis=1).astype(BF16)
            product = jnp.dot(tiles, keys[part, pl.ds(k * depth, depth)], preferred_element_type=F32)
            totals[part] = product if totals[part] is None else totals[part] + product

    multiply(3)
    send_far(3)
    multiply(0)
    send_far(0)
    multiply(1)
    send_far(1)
    multiply(2)
    send_far(2)
    send_near(0)
    pass_on(0)
    send_near(1)
    pl.semaphore_wait(across_sem, 1)
    for target in (right, left):
        pl.semaphore_signal(plane_sem, inc=1, device_id=target, device_id_type=MESH)
    pass_on(1)
    send_near(2)
    pass_on(2)
    pl.semaphore_wait(plane_sem, 2)
    direct((0,))
    direct((1, 2))
    to_owners(0)
    to_owners(1)
    to_owners(2)
    keys_copy.wait()
    sent.append(db_swap)
    for copies in (far_copies, near_copies):
        sent.extend(copies.values())
    for copy in sent:
        copy.wait_send()
    pack(0)
    pack(1)
    pack(2)
    finish_sends(range(STAGED))
    for origin in range(3):
        block = direct_out.at[origin] if origin else direct_out.at[0, pl.ds(1, 15)]
        pltpu.make_async_copy(block, block, direct_sems.at[0, origin]).wait()
    pack(3)
    for part in range(2):
        out_ref[part] = totals[part]


def shards(database, query, slot_map, keys):
    rows_axis = lax.axis_size("row")
    factor = float(database.shape[0] * rows_axis) ** (-0.5)
    total = slot_map.shape[0]
    rows, columns = database.shape
    tile, packs = keys.shape[1:]
    width = columns // CHUNKS
    half = total // 2
    dma = pltpu.SemaphoreType.DMA
    return pl.pallas_call(
        functools.partial(kernel, factor),
        out_shape=jax.ShapeDtypeStruct((2, 16, packs), F32),
        in_specs=[pl.BlockSpec(memory_space=pltpu.HBM)] * 4,
        out_specs=pl.BlockSpec(memory_space=pltpu.VMEM),
        scratch_shapes=[
            pltpu.VMEM((1, total), jnp.int32),
            pltpu.VMEM((8, total // 8, rows), BF16),
            pltpu.VMEM((2, rows, columns), BF16),
            pltpu.VMEM((2, tile, packs), BF16),
            pltpu.VMEM((half, rows), BF16),
            pltpu.VMEM((half, rows), BF16),
            pltpu.VMEM((CHUNKS, half, width), F32),
            pltpu.VMEM((CHUNKS, 2, 16, width), BF16),
            pltpu.VMEM((CHUNKS, 2, 16, width), BF16),
            pltpu.VMEM((STAGED, 2, 2, 16, width), BF16),
            pltpu.VMEM((STAGED, 2, 2, 16, width), BF16),
            pltpu.VMEM((tile // CHUNKS // 128 * 64, 128), F32),
            pltpu.VMEM((STAGED, 16, tile // CHUNKS // 32, 128), BF16),
            pltpu.VMEM((STAGED, 2, 8, tile // CHUNKS // 32, 128), BF16),
            pltpu.VMEM((tile // CHUNKS // 128 * 32, 128), F32),
            dma((2,)),
            dma(()),
            dma((2,)),
            dma(()),
            dma((2, 7)),
            dma((2,)),
            dma((2, CHUNKS, 2)),
            dma((2, STAGED, 2, 2)),
            dma((2, STAGED)),
            pltpu.VMEM((3, 16, CHUNKS - STAGED, tile // CHUNKS // 32, 128), BF16),
            pltpu.VMEM((3, 2, 8, CHUNKS - STAGED, tile // CHUNKS // 32, 128), BF16),
            dma((2, 3)),
            pltpu.SemaphoreType.REGULAR,
            pltpu.SemaphoreType.REGULAR,
        ],
        compiler_params=pltpu.CompilerParams(
            collective_id=1, has_side_effects=True, vmem_limit_bytes=40 * 1024 * 1024
        ),
        name="answer_and_pack",
    )(*(pltpu.with_memory_space_constraint(a, pltpu.HBM) for a in (slot_map.reshape(1, total), query, database, keys)))


def solution(mesh):
    return jax.shard_map(
        shards,
        mesh=mesh,
        in_specs=(P("row", "col"), P("col", "row"), P(), P(("row", "col"), None, None)),
        out_specs=P(("row", "col"), None, None),
        check_vma=False,
    )
```

```python
import functools

import jax
import jax.numpy as jnp
from jax import lax
from jax.experimental import pallas as pl
from jax.experimental.pallas import tpu as pltpu
from jax.sharding import PartitionSpec as P

MESH = pl.DeviceIdType.MESH
CHUNKS = 4
STAGED = 3
F32 = jnp.float32
BF16 = jnp.bfloat16


def place():
    row, col = lax.axis_index("row"), lax.axis_index("col")
    x, y_hi, core = row // 4, lax.rem(row // 2, 2), lax.rem(row, 2)
    z, y_lo = col // 2, lax.rem(col, 2)
    return x, 2 * y_hi + y_lo, z, core


def device(x, y, z, core):
    x, y, z = lax.rem(x, 4), lax.rem(y, 4), lax.rem(z, 4)
    return ((2 * x + y // 2) * 2 + core, 2 * z + lax.rem(y, 2))


def kernel(
    factor,
    slot_hbm,
    query_hbm,
    db_hbm,
    keys_hbm,
    out_ref,
    slots,
    gathered,
    db,
    keys,
    my_lines,
    their_lines,
    own,
    far_out,
    far_in,
    near_out,
    near_in,
    spread,
    send_out,
    arrived,
    switched,
    local_sem,
    db_sem,
    db_sems,
    keys_sem,
    query_sems,
    core_sems,
    far_sems,
    near_sems,
    owner_sems,
    direct_out,
    direct_in,
    direct_sems,
    across_sem,
    plane_sem,
):
    x, y, z, core = place()
    y_hi, y_lo = y // 2, lax.rem(y, 2)
    col = 2 * z + y_lo
    depth = keys_hbm.shape[1] // CHUNKS
    lane_groups = depth // 128

    def remote(src, dst, sems, index, target):
        return pltpu.make_async_remote_copy(
            src_ref=src,
            dst_ref=dst,
            send_sem=sems.at[(0, *index)],
            recv_sem=sems.at[(1, *index)],
            device_id=target,
            device_id_type=MESH,
        )

    partner = device(x, y, z, 1 - core)
    right, left = device(x + 1, y, z, core), device(x + 3, y, z, core)
    owners = [device(x, y + b // 4, z + b % 4, core) for b in range(16)]
    column_peers = []
    for dz, other in ((2, 1), (2, 0), (1, 1), (3, 1), (1, 0), (3, 0), (0, 1)):
        peer_y = 2 * y_hi + (1 - y_lo if other else y_lo)
        column_peers.append(device(x, peer_y, z + dz, core))
    across = device(x, y + 3 + 2 * y_lo, z, core)

    barrier = pltpu.get_barrier_semaphore()
    greeted = [*column_peers, across, partner, right, left]
    for target in greeted:
        pl.semaphore_signal(barrier, inc=1, device_id=target, device_id_type=MESH)
    pl.semaphore_wait(barrier, len(greeted))

    query_copies = []
    for i, target in enumerate(column_peers):
        copy = remote(query_hbm, gathered.at[col], query_sems, (i,), target)
        copy.start()
        query_copies.append(copy)

    slot_copy = pltpu.make_async_copy(slot_hbm, slots, local_sem.at[0])
    slot_copy.start()
    own_query = pltpu.make_async_copy(query_hbm, gathered.at[col], local_sem.at[1])
    own_query.start()
    db_swap = remote(db_hbm, db.at[1], db_sems, (), partner)
    db_swap.start()
    db_copy = pltpu.make_async_copy(db_hbm, db.at[0], db_sem)
    db_copy.start()
    keys_copy = pltpu.make_async_copy(keys_hbm, keys, keys_sem)
    keys_copy.start()

    slot_copy.wait()
    total = slots.shape[1]
    line = lax.broadcasted_iota(jnp.int32, (total, total), 0)
    place_at = lax.broadcasted_iota(jnp.int32, (total, total), 1)
    to_core = (line >> 7) + core & 1
    to_x = (line >> 5) + x & 3
    part = line >> 4 & 1
    to_y = (line >> 2) + y & 3
    to_z = line + z & 3
    owner_row = (to_x * 2 + (to_y >> 1)) * 2 + to_core
    owner_col = to_z * 2 + (to_y & 1)
    slot_of_line = (owner_row * 8 + owner_col) * 2 + part
    line_is_slot = jnp.where(slot_of_line == place_at, 1.0, 0.0).astype(BF16)
    client_at_slot = jnp.broadcast_to(slots[...], (total, total))
    client_is_slot = jnp.where(client_at_slot == line, 1.0, 0.0).astype(BF16)
    chooser = lax.dot_general(
        line_is_slot, client_is_slot, (((1,), (1,)), ((), ())), preferred_element_type=F32
    ).astype(BF16)

    own_query.wait()
    for copy in query_copies:
        copy.wait_recv()
    entries = gathered[...].reshape(total, query_hbm.shape[1])
    half = total // 2

    def choose(lines):
        return jnp.dot(lines, entries, preferred_element_type=F32).astype(BF16)

    sent = list(query_copies)
    far_copies, near_copies = {}, {}
    my_lines[...] = choose(chooser[half:])
    lines_copy = remote(my_lines, their_lines, core_sems, (), partner)
    lines_copy.start()
    pl.semaphore_signal(across_sem, inc=1, device_id=across, device_id_type=MESH)
    own_lines = choose(chooser[:half])
    sent.append(lines_copy)
    db_copy.wait()
    db_swap.wait_recv()
    lines_copy.wait_recv()
    both_lines = jnp.concatenate([own_lines, their_lines[...]], axis=1)

    def multiply(k):
        for t in range(2):
            start = t * keys_hbm.shape[1] + k * depth
            block = db[:, :, start : start + depth]
            own[k, :, t * depth : (t + 1) * depth] = jnp.dot(
                both_lines,
                block.reshape(db.shape[0] * db.shape[1], depth),
                preferred_element_type=F32,
            )

    def start_near(k, side, lines):
        target = (right, left)[side]
        copy = remote(
            near_out.at[k, side, lines],
            near_in.at[k, side, lines],
            near_sems,
            (k, side, lines),
            target,
        )
        copy.start()
        near_copies[k, side, lines] = copy

    def send_far(k):
        for side in range(2):
            far_out[k, side] = own[k, pl.ds(64 + 16 * side, 16)].astype(BF16)
            copy = remote(
                far_out.at[k, side], far_in.at[k, side], far_sems, (k, side), (right, left)[side]
            )
            copy.start()
            far_copies[k, side] = copy

    def send_near(k):
        for side in range(2):
            near_out[k, side, 1 - side] = own[k, pl.ds((48, 96)[side], 16)].astype(BF16)
            start_near(k, side, 1 - side)

    def pass_on(k):
        for side in range(2):
            far_copies[k, side].wait_recv()
            lines = pl.ds((32, 112)[side], 16)
            near_out[k, side, side] = (own[k, lines] + far_in[k, side].astype(F32)).astype(BF16)
            start_near(k, side, side)

    far_first = sorted(range(16), key=lambda b: -min(b // 4, 4 - b // 4) - min(b % 4, 4 - b % 4))

    def to_owners(k):
        for part in range(2):
            for side in range(2):
                near_copies[k, side, part].wait_recv()
            lines = pl.ds(16 * part, 16)
            summed = (
                own[k, lines] + near_in[k, 0, part].astype(F32) + near_in[k, 1, part].astype(F32)
            )
            for t in range(2):
                for g in range(lane_groups):
                    lane = t * depth + g * 128
                    at = t * 2 * lane_groups + part * lane_groups + g
                    spread[pl.ds(at, 16, stride=4 * lane_groups), :] = summed[:, lane : lane + 128]
        send_out[k] = spread[...].astype(BF16).reshape(send_out.shape[1:])
        landing = arrived.at[k, y_hi, col]
        for b in far_first[:-1]:
            remote(send_out.at[k, b], landing, owner_sems, (k,), owners[b]).start()
        pltpu.make_async_copy(send_out.at[k, 0], landing, owner_sems.at[1, k]).start()

    def direct(origins):
        for origin in origins:
            for k in range(STAGED, CHUNKS):
                side = origin - 1
                if origin:
                    far_copies[k, side].wait_recv()
                for part in range(2):
                    summed = own[k, pl.ds((0, 32, 96)[origin] + 16 * part, 16)]
                    if origin and part == side:
                        summed = summed + far_in[k, side].astype(F32)
                    for t in range(2):
                        for g in range(lane_groups):
                            lane = t * depth + g * 128
                            at = t * 2 * lane_groups + part * lane_groups + g
                            spread[pl.ds(at, 16, stride=4 * lane_groups), :] = summed[
                                :, lane : lane + 128
                            ]
                direct_out[origin, :, k - STAGED] = spread[...].astype(BF16).reshape(
                    16, *direct_out.shape[3:]
                )
        for b in far_first:
            for origin in origins:
                landing = direct_in.at[origin, y_hi, col]
                if b or origin:
                    target = device(x + (0, 1, 3)[origin], y + b // 4, z + b % 4, core)
                    remote(direct_out.at[origin, b], landing, direct_sems, (origin,), target).start()
                else:
                    pltpu.make_async_copy(
                        direct_out.at[0, 0], landing, direct_sems.at[1, 0]
                    ).start()

    totals = [None, None]

    def finish_sends(chunks):
        for k in chunks:
            block = send_out.at[k, pl.ds(1, 15)]
            pltpu.make_async_copy(block, block, owner_sems.at[0, k]).wait()


    def pack(k):
        if k < STAGED:
            pltpu.make_async_copy(arrived.at[k], arrived.at[k], owner_sems.at[1, k]).wait()
            both = arrived[k, 0].astype(F32) + arrived[k, 1].astype(F32)
        else:
            both = None
            for origin in (0, 1, 2):
                block = direct_in.at[origin]
                if k == STAGED:
                    pltpu.make_async_copy(block, block, direct_sems.at[1, origin]).wait()
                pair = direct_in[origin, 0, :, k - STAGED].astype(F32)
                pair = pair + direct_in[origin, 1, :, k - STAGED].astype(F32)
                both = pair if both is None else both + pair
        switched[...] = (both * factor).reshape(switched.shape)
        for part in range(2):
            pieces = [
                switched[pl.ds(part * lane_groups + g, 16, stride=2 * lane_groups), :]
                for g in range(lane_groups)
            ]
            tiles = jnp.concatenate(pieces, axis=1).astype(BF16)
            product = jnp.dot(tiles, keys[part, pl.ds(k * depth, depth)], preferred_element_type=F32)
            totals[part] = product if totals[part] is None else totals[part] + product

    multiply(3)
    send_far(3)
    multiply(0)
    send_far(0)
    multiply(1)
    send_far(1)
    multiply(2)
    send_far(2)
    send_near(0)
    pass_on(0)
    send_near(1)
    pl.semaphore_wait(across_sem, 1)
    for target in (right, left):
        pl.semaphore_signal(plane_sem, inc=1, device_id=target, device_id_type=MESH)
    pass_on(1)
    send_near(2)
    pass_on(2)
    direct((0,))
    pl.semaphore_wait(plane_sem, 2)
    direct((1, 2))
    to_owners(0)
    to_owners(1)
    to_owners(2)
    keys_copy.wait()
    sent.append(db_swap)
    for copies in (far_copies, near_copies):
        sent.extend(copies.values())
    for copy in sent:
        copy.wait_send()
    pack(0)
    pack(1)
    pack(2)
    finish_sends(range(STAGED))
    for origin in range(3):
        block = direct_out.at[origin] if origin else direct_out.at[0, pl.ds(1, 15)]
        pltpu.make_async_copy(block, block, direct_sems.at[0, origin]).wait()
    pack(3)
    for part in range(2):
        out_ref[part] = totals[part]


def shards(database, query, slot_map, keys):
    rows_axis = lax.axis_size("row")
    factor = float(database.shape[0] * rows_axis) ** (-0.5)
    total = slot_map.shape[0]
    rows, columns = database.shape
    tile, packs = keys.shape[1:]
    width = columns // CHUNKS
    half = total // 2
    dma = pltpu.SemaphoreType.DMA
    return pl.pallas_call(
        functools.partial(kernel, factor),
        out_shape=jax.ShapeDtypeStruct((2, 16, packs), F32),
        in_specs=[pl.BlockSpec(memory_space=pltpu.HBM)] * 4,
        out_specs=pl.BlockSpec(memory_space=pltpu.VMEM),
        scratch_shapes=[
            pltpu.VMEM((1, total), jnp.int32),
            pltpu.VMEM((8, total // 8, rows), BF16),
            pltpu.VMEM((2, rows, columns), BF16),
            pltpu.VMEM((2, tile, packs), BF16),
            pltpu.VMEM((half, rows), BF16),
            pltpu.VMEM((half, rows), BF16),
            pltpu.VMEM((CHUNKS, half, width), F32),
            pltpu.VMEM((CHUNKS, 2, 16, width), BF16),
            pltpu.VMEM((CHUNKS, 2, 16, width), BF16),
            pltpu.VMEM((STAGED, 2, 2, 16, width), BF16),
            pltpu.VMEM((STAGED, 2, 2, 16, width), BF16),
            pltpu.VMEM((tile // CHUNKS // 128 * 64, 128), F32),
            pltpu.VMEM((STAGED, 16, tile // CHUNKS // 32, 128), BF16),
            pltpu.VMEM((STAGED, 2, 8, tile // CHUNKS // 32, 128), BF16),
            pltpu.VMEM((tile // CHUNKS // 128 * 32, 128), F32),
            dma((2,)),
            dma(()),
            dma((2,)),
            dma(()),
            dma((2, 7)),
            dma((2,)),
            dma((2, CHUNKS, 2)),
            dma((2, STAGED, 2, 2)),
            dma((2, STAGED)),
            pltpu.VMEM((3, 16, CHUNKS - STAGED, tile // CHUNKS // 32, 128), BF16),
            pltpu.VMEM((3, 2, 8, CHUNKS - STAGED, tile // CHUNKS // 32, 128), BF16),
            dma((2, 3)),
            pltpu.SemaphoreType.REGULAR,
            pltpu.SemaphoreType.REGULAR,
        ],
        compiler_params=pltpu.CompilerParams(
            collective_id=1, has_side_effects=True, vmem_limit_bytes=40 * 1024 * 1024
        ),
        name="answer_and_pack",
    )(*(pltpu.with_memory_space_constraint(a, pltpu.HBM) for a in (slot_map.reshape(1, total), query, database, keys)))


def solution(mesh):
    return jax.shard_map(
        shards,
        mesh=mesh,
        in_specs=(P("row", "col"), P("col", "row"), P(), P(("row", "col"), None, None)),
        out_specs=P(("row", "col"), None, None),
        check_vma=False,
    )
```
